32 devices in a mesh: wide: 8 (over y, x, core), narrow: 4 (over z).
Axes of the slice: x: 2, y: 2, z: 4, core: 2. Of those that a mesh axis runs over, the one named last changes fastest.
Arguments:
- start_field: float32 [64, 16384], P(None, ('wide', 'narrow')), may hold values from -6 to 6
- right_side: float32 [64, 16384], P(None, ('wide', 'narrow')), may hold values from -6 to 6
- element_scale: float32 [16384], P(('wide', 'narrow')), may hold values from 2 to 6
- face_scale: float32 [6, 16384], P(None, ('wide', 'narrow')), may hold values from 0.1 to 0.6
- face_nbr: int32 [6, 16384], P(None, ('wide', 'narrow')), may hold values from -1 to 767, as said below
- send_list: int32 [4, 2048], P(None, ('wide', 'narrow')), may hold values from 0 to 511, as said below
- counts: int32 [32], P(('wide', 'narrow')), may hold values from 256 to 512, as said below
- coarse_slot: int32 [16384], P(('wide', 'narrow')), may hold values from 0 to 511, as said below
- elem_block: float32 [64, 64], replicated, may hold values from -1.5 to 1.5
- smooth_block: float32 [64, 64], replicated, may hold values from -1.5 to 1.5
- face_blocks: float32 [6, 64, 64], replicated, may hold values from -0.375 to 0.375
- prolong: float32 [8, 64, 8], replicated, may hold values from -1 to 1
- coarse_scale: float32 [2048], P(('wide', 'narrow')), may hold values from 2 to 6
- coarse_face_scale: float32 [6, 2048], P(None, ('wide', 'narrow')), may hold values from 0.1 to 0.6
- coarse_nbr: int32 [6, 2048], P(None, ('wide', 'narrow')), may hold values from -1 to 127, as said below
- coarse_send: int32 [4, 512], P(None, ('wide', 'narrow')), may hold values from 0 to 63, as said below
- coarse_block: float32 [8, 8], replicated, may hold values from -1.5 to 1.5
- coarse_smooth: float32 [8, 8], replicated, may hold values from -1.5 to 1.5
- coarse_faces: float32 [6, 8, 8], replicated, may hold values from -0.9 to 0.9
Outputs:
- smoothed_field: float32 [64, 16384], P(None, ('wide', 'narrow'))
- coarse_correction: float32 [8, 2048], P(None, ('wide', 'narrow'))
The draws below stay inside these ranges and needn't reach their ends.
Inputs may be any that keep to these rules, and one draw needn't show every extreme that they name: `face_nbr`: -1 marks a face without neighbour; a value below 512 names a slot of the same partition; 512 + d * 64 + j names the j-th element sent by the neighbouring partition in direction d. Each partition names every value from 512 to 767 on some face. `send_list`: row d holds, for each partition, 64 distinct local slots: row 0 goes to the partition one higher on wide, row 1 one lower on wide, rows 2 and 3 likewise on narrow, cyclically. `counts`: one partition has 512 active elements and one has 256. `coarse_slot`: within each partition a permutation of 0 to 511. `coarse_nbr`: as face_nbr, with 64 coarse elements and 16 sent in each direction. `coarse_send`: as send_list, 16 distinct local coarse elements for each partition and direction.
All inputs are finite; a program needn't handle non-finite values.
Results may differ from the reference program's by a relative error of at most 0.0003.
Values sent between devices are 32-bit elements; how exact they have to be, the bound alone decides.
No kernel may reach another device: no remote copies, remote signals or barrier semaphores. Data moves between devices by JAX's collectives and lax.ppermute only.
A program may use at most 64 MiB of HBM per device.

```python
import math
import jax
import jax.numpy as jnp
from jax import lax

DOF = 64
CDOF = 8
E = 512
CS = 3
B = 64
NC = 64
SB = 16
PW = 8
PN = 4
DEVS = 32
NELEM = 16384
NCTOT = 2048


def neighbour_table(key, local_count, send_count):
    total = local_count * DEVS
    key_kind, key_near, key_far, key_cover = jax.random.split(key, 4)
    kinds = jax.random.randint(key_kind, (6, total), 0, 20)
    nearby = jax.random.randint(key_near, (6, total), 0, local_count)
    remote = jax.random.randint(key_far, (6, total), local_count, local_count + 4 * send_count)
    table = jnp.where(kinds < 3, remote, jnp.where(kinds == 3, -1, nearby))
    cover_keys = jax.random.split(key_cover, DEVS)
    picks = jax.vmap(lambda subkey: jax.random.permutation(subkey, local_count)[:4 * send_count])(cover_keys)
    columns = (jnp.arange(DEVS)[:, None] * local_count + picks).reshape(-1)
    values = jnp.tile(local_count + jnp.arange(4 * send_count), DEVS)
    table = table.at[5, columns].set(values)
    return table.astype(jnp.int32)


def send_table(key, local_count, send_count):
    keys = jax.random.split(key, 4 * DEVS)
    picks = jax.vmap(lambda subkey: jax.random.permutation(subkey, local_count)[:send_count])(keys)
    return picks.reshape(4, DEVS * send_count).astype(jnp.int32)


def dominant(key, order, spread):
    key_diag, key_off = jax.random.split(key)
    diagonal = jax.random.uniform(key_diag, (order,), jnp.float32, 0.8, 1.2)
    offdiag = jnp.clip(jax.random.normal(key_off, (order, order), jnp.float32), -4.0, 4.0) * spread
    identity = jnp.eye(order, dtype=jnp.float32)
    return (offdiag * (1.0 - identity) + identity * diagonal[None, :]).astype(jnp.float32)


def draw_face_nbr(key, part):
    return neighbour_table(jax.random.fold_in(key, 11), E, B)


def draw_send_list(key, part):
    return send_table(jax.random.fold_in(key, 12), E, B)


def draw_coarse_nbr(key, part):
    return neighbour_table(jax.random.fold_in(key, 13), NC, SB)


def draw_coarse_send(key, part):
    return send_table(jax.random.fold_in(key, 14), NC, SB)


def draw_counts(key, part):
    key_count, key_order = jax.random.split(jax.random.fold_in(key, 15))
    values = jax.random.randint(key_count, (DEVS,), E // 2, E + 1)
    order = jax.random.permutation(key_order, DEVS)
    values = values.at[order[0]].set(E).at[order[1]].set(E // 2)
    return values.astype(jnp.int32)


def draw_coarse_slot(key, part):
    keys = jax.random.split(jax.random.fold_in(key, 16), DEVS)
    picks = jax.vmap(lambda subkey: jax.random.permutation(subkey, E))(keys)
    return picks.reshape(-1).astype(jnp.int32)


def draw_elem_block(key, part):
    return dominant(jax.random.fold_in(key, 21), DOF, 0.04)


def draw_smooth_block(key, part):
    return dominant(jax.random.fold_in(key, 22), DOF, 0.04)


def draw_coarse_block(key, part):
    return dominant(jax.random.fold_in(key, 23), CDOF, 0.12)


def draw_coarse_smooth(key, part):
    return dominant(jax.random.fold_in(key, 24), CDOF, 0.12)


def shard_levels(key, dims, cuts, least, largest):
    def one(dim, shards_of):
        heights = jax.random.uniform(jax.random.fold_in(jax.random.fold_in(key, 6), dim), (shards_of,), jnp.float32, least / len(cuts), largest / len(cuts))
        return jnp.repeat(jnp.exp(heights), dims[dim] // shards_of).reshape((-1,) + (1,) * (len(dims) - dim - 1))

    loudness = one(*cuts[0])
    for cut in cuts[1:]:
        loudness = loudness * one(*cut)
    return loudness


def scatter_about(stream_key, dims, scale, bound, cuts=(), kind=jnp.bfloat16):
    loudness = shard_levels(stream_key, dims, cuts, -0.22, 0.18) if cuts else 1.0
    values = jax.random.normal(stream_key, dims, jnp.float32) * scale * loudness
    return jnp.minimum(jnp.maximum(values, -bound), bound).astype(kind)


def setup_inputs(seed: int = 0) -> dict:
    arg_keys = jax.random.split(jax.random.key(seed), 20)
    return {
        "start_field": scatter_about(arg_keys[0], (DOF, NELEM), 1.0, 6.0, ((1, 32),), jnp.float32),
        "right_side": scatter_about(arg_keys[1], (DOF, NELEM), 1.0, 6.0, ((1, 32),), jnp.float32),
        "element_scale": jnp.clip(jnp.exp(math.log(6.0) - 1.0986123 * jax.random.uniform(arg_keys[2], (NELEM,), jnp.float32) ** shard_levels(arg_keys[2], (NELEM,), ((0, 32),), -0.2, 0.2)), 2.0, 6.0),
        "face_scale": jnp.clip(jnp.exp(math.log(0.6) - 1.7917595 * jax.random.uniform(arg_keys[3], (6, NELEM), jnp.float32) ** shard_levels(arg_keys[3], (6, NELEM), ((1, 32),), -0.2, 0.2)), 0.1, 0.6),
        "face_nbr": draw_face_nbr(jax.random.fold_in(arg_keys[19], 71), 0),
        "send_list": draw_send_list(jax.random.fold_in(arg_keys[19], 71), 0),
        "counts": draw_counts(jax.random.fold_in(arg_keys[19], 71), 0),
        "coarse_slot": draw_coarse_slot(jax.random.fold_in(arg_keys[19], 71), 0),
        "elem_block": draw_elem_block(jax.random.fold_in(arg_keys[19], 71), 0),
        "smooth_block": draw_smooth_block(jax.random.fold_in(arg_keys[19], 71), 0),
        "face_blocks": scatter_about(arg_keys[10], (6, DOF, DOF), 0.0625, 0.375, (), jnp.float32),
        "prolong": scatter_about(arg_keys[11], (8, DOF, CDOF), 32 ** -0.5, 1.0, (), jnp.float32),
        "coarse_scale": jnp.clip(jnp.exp(math.log(6.0) - 1.0986123 * jax.random.uniform(arg_keys[12], (NCTOT,), jnp.float32) ** shard_levels(arg_keys[12], (NCTOT,), ((0, 32),), -0.2, 0.2)), 2.0, 6.0),
        "coarse_face_scale": jnp.clip(jnp.exp(math.log(0.6) - 1.7917595 * jax.random.uniform(arg_keys[13], (6, NCTOT), jnp.float32) ** shard_levels(arg_keys[13], (6, NCTOT), ((1, 32),), -0.2, 0.2)), 0.1, 0.6),
        "coarse_nbr": draw_coarse_nbr(jax.random.fold_in(arg_keys[19], 71), 0),
        "coarse_send": draw_coarse_send(jax.random.fold_in(arg_keys[19], 71), 0),
        "coarse_block": draw_coarse_block(jax.random.fold_in(arg_keys[19], 71), 0),
        "coarse_smooth": draw_coarse_smooth(jax.random.fold_in(arg_keys[19], 71), 0),
        "coarse_faces": scatter_about(arg_keys[18], (6, CDOF, CDOF), 0.15, 0.9, (), jnp.float32),
    }


OMEGA = 0.7
COARSE_OMEGA = 0.6
HIGH = lax.Precision.HIGHEST


def product(left, right):
    return jnp.dot(left, right, preferred_element_type=jnp.float32, precision=HIGH)


def neighbour_index(table, sends, local_count, send_count):
    total = table.shape[1]
    element = jnp.arange(total, dtype=jnp.int32)
    owner = element // local_count
    wide_pos = owner // PN
    narrow_pos = owner % PN
    sources = jnp.stack([((wide_pos - 1) % PW) * PN + narrow_pos,
                         ((wide_pos + 1) % PW) * PN + narrow_pos,
                         wide_pos * PN + (narrow_pos - 1) % PN,
                         wide_pos * PN + (narrow_pos + 1) % PN])
    targets = []
    for face_index in range(6):
        entry = table[face_index]
        ghost = jnp.clip(entry - local_count, 0, 4 * send_count - 1)
        direction = ghost // send_count
        offset = ghost % send_count
        source = jnp.take_along_axis(sources, direction[None, :], axis=0)[0]
        remote = sends[direction, source * send_count + offset]
        target = jnp.where(entry < local_count, owner * local_count + entry, source * local_count + remote)
        targets.append(jnp.where(entry < 0, -1, target))
    return jnp.stack(targets).astype(jnp.int32)


def apply_operator(current, scale, face_scale, table, block, faces):
    result = scale[None, :] * product(block, current)
    for face_index in range(6):
        target = table[face_index]
        weight = jnp.where(target >= 0, face_scale[face_index], 0.0)
        gathered = jnp.take(current, jnp.maximum(target, 0), axis=1)
        result = result + weight[None, :] * product(faces[face_index], gathered)
    return result


def smooth_step(current, residual, active, scale, block):
    return current + OMEGA * active[None, :] * product(block, residual) / scale[None, :]


def reference(start_field, right_side, element_scale, face_scale, face_nbr, send_list, counts, coarse_slot,
              elem_block, smooth_block, face_blocks, prolong, coarse_scale, coarse_face_scale, coarse_nbr,
              coarse_send, coarse_block, coarse_smooth, coarse_faces):
    rows = start_field.shape[0]
    total = start_field.shape[1]
    element = jnp.arange(total, dtype=jnp.int32)
    owner = element // E
    active = ((element % E) < counts[owner]).astype(jnp.float32)
    fine_index = neighbour_index(face_nbr, send_list, E, B)
    coarse_index = neighbour_index(coarse_nbr, coarse_send, NC, SB)
    start = start_field * active[None, :]
    source = right_side * active[None, :]

    def fine_apply(current):
        return apply_operator(current, element_scale, face_scale, fine_index, elem_block, face_blocks)

    def coarse_apply(current):
        return apply_operator(current, coarse_scale, coarse_face_scale, coarse_index, coarse_block, coarse_faces)

    first_residual = source - fine_apply(start)
    smoothed = smooth_step(start, first_residual, active, element_scale, smooth_block)
    fine_residual = source - fine_apply(smoothed)
    slots = (owner * E + coarse_slot).astype(jnp.int32)
    ordered = jnp.zeros_like(fine_residual).at[:, slots].set(fine_residual)
    ordered = ordered.reshape(rows, total // 8, 8)
    coarse_rhs = jnp.einsum("kij,ick->jc", prolong, ordered, precision=HIGH)
    correction = COARSE_OMEGA * product(coarse_smooth, coarse_rhs) / coarse_scale[None, :]
    for sweep_index in range(CS - 1):
        correction = correction + COARSE_OMEGA * product(coarse_smooth, coarse_rhs - coarse_apply(correction)) / coarse_scale[None, :]
    expanded = jnp.einsum("kij,jc->ick", prolong, correction, precision=HIGH).reshape(rows, total)
    corrected = smoothed + active[None, :] * jnp.take(expanded, slots, axis=1)
    final_residual = source - fine_apply(corrected)
    smoothed_field = smooth_step(corrected, final_residual, active, element_scale, smooth_block)
    return smoothed_field, correction
```

```python
import functools

import jax
import jax.numpy as jnp
from jax import lax
from jax.experimental import pallas as pl
from jax.experimental.pallas import tpu as pltpu
from jax.sharding import PartitionSpec as P

OMEGA = 0.7
COARSE_OMEGA = 0.6
HIGH = lax.Precision.HIGHEST
LANES = 128
SUB = 8
FACES = 6
SF_W, RF_W, SF_N, RF_N, AT_W, AT_N = range(6)


def dot(left, right):
    return jnp.dot(left, right, preferred_element_type=jnp.float32, precision=HIGH)


def dot_t(left, right):
    return lax.dot_general(
        left, right, (((1,), (1,)), ((), ())), preferred_element_type=jnp.float32, precision=HIGH
    )


def lane_take(tile, index):
    return jnp.take_along_axis(tile, index, axis=1, mode="promise_in_bounds")


def pick(tiles, index):
    low = index & (LANES - 1)
    high = index >> 7
    found = lane_take(tiles[0], low)
    for place in range(1, len(tiles)):
        found = jnp.where(high == place, lane_take(tiles[place], low), found)
    return found


def rows8(row):
    return jnp.broadcast_to(row, (SUB, row.shape[1]))


def by_flag(flag, one, other):
    return jnp.where(flag != 0, one, other)


def activity(counts_ref, elements):
    lane = lax.broadcasted_iota(jnp.int32, (1, elements), 1)
    return lane < counts_ref[0]


def ordered_sends(flags_ref, send):
    out = []
    for base, flag in ((0, SF_W), (2, SF_N)):
        first, second = send[base : base + 1], send[base + 1 : base + 2]
        out.append(by_flag(flags_ref[flag], second, first))
        out.append(by_flag(flags_ref[flag], first, second))
    return out


def store_packets(outs, halves, row):
    size = outs[0].shape[1]
    for half, tile in enumerate(halves):
        outs[2 * half][row : row + SUB, :] = tile[:, :size]
        outs[2 * half + 1][row : row + SUB, :] = tile[:, size : 2 * size]


def pack(flags_ref, send, source_ref, outs, rows, elements):
    order = ordered_sends(flags_ref, send)
    index = [rows8(jnp.concatenate(order[:2], axis=1)), rows8(jnp.concatenate(order[2:], axis=1))]
    for row in range(0, rows, SUB):
        tiles = [source_ref[row : row + SUB, c : c + LANES] for c in range(0, elements, LANES)]
        store_packets(outs, [pick(tiles, which) for which in index], row)
    return index


def received(flags_ref, packets, row):
    tiles = []
    for base, flag in ((0, RF_W), (2, RF_N)):
        first = packets[base][row : row + SUB, :]
        second = packets[base + 1][row : row + SUB, :]
        tiles.append(
            jnp.concatenate(
                [by_flag(flags_ref[flag], second, first), by_flag(flags_ref[flag], first, second)], axis=1
            )
        )
    return tiles


def start_kernel(flags_ref, counts_ref, start_ref, slot_ref, send_ref, csend_ref, masked_ref, *outs):
    rows, elements = start_ref.shape
    active = activity(counts_ref, elements)
    masked_ref[...] = jnp.where(active, start_ref[...], 0.0)
    index = pack(flags_ref, send_ref[...], masked_ref, outs, rows, elements)
    slots = rows8(jnp.where(active, slot_ref[...], -1).astype(jnp.float32))
    tiles = [slots[:, c : c + LANES] for c in range(0, elements, LANES)]
    csend = csend_ref[...].astype(jnp.float32)
    blank = jnp.zeros((1, LANES // 2 - csend.shape[1]), jnp.float32)
    order = ordered_sends(flags_ref, csend)
    line = lax.broadcasted_iota(jnp.int32, (SUB, LANES), 0)
    halves = []
    for half in range(2):
        coarse = jnp.concatenate([order[2 * half], blank, order[2 * half + 1], blank], axis=1)
        halves.append(jnp.where(line == 0, pick(tiles, index[half]), rows8(coarse)))
    store_packets(outs, halves, rows)


def local_blocks(current_ref, scale_ref, fscale_ref, nbr_ref, g_ref):
    rows, elements = current_ref.shape
    for c in range(0, elements, LANES):
        cols = slice(c, c + LANES)
        g_ref[0:rows, cols] = current_ref[:, cols] * scale_ref[:, cols]
    for face in range(FACES):
        for c in range(0, elements, LANES):
            cols = slice(c, c + LANES)
            entry = nbr_ref[face : face + 1, cols]
            here = (entry >= 0) & (entry < elements)
            weight = rows8(jnp.where(here, fscale_ref[face : face + 1, cols], 0.0))
            index = rows8(jnp.where(here, entry, 0))
            for row in range(0, rows, SUB):
                tiles = [current_ref[row : row + SUB, k : k + LANES] for k in range(0, elements, LANES)]
                at = rows * (face + 1) + row
                g_ref[at : at + SUB, cols] = weight * pick(tiles, index)


def ghost_blocks(flags_ref, packets, rows, elements, fscale_ref, nbr_ref, g_ref):
    halves = [received(flags_ref, packets, row) for row in range(0, rows, SUB)]
    for face in range(FACES):
        for c in range(0, elements, LANES):
            cols = slice(c, c + LANES)
            entry = nbr_ref[face : face + 1, cols]
            there = entry >= elements
            weight = rows8(jnp.where(there, fscale_ref[face : face + 1, cols], 0.0))
            index = rows8(jnp.where(there, entry - elements, 0))
            for row in range(0, rows, SUB):
                at = rows * face + row
                g_ref[at : at + SUB, cols] = weight * pick(halves[row // SUB], index)


def first_local_kernel(
    counts_ref,
    start_ref,
    right_ref,
    scale_ref,
    fscale_ref,
    nbr_ref,
    elem_ref,
    smooth_ref,
    faces_ref,
    prolong_ref,
    csmooth_ref,
    part_ref,
    folded_ref,
    lead_ref,
    relax_ref,
    source_ref,
    g_ref,
):
    rows, elements = start_ref.shape
    active = activity(counts_ref, elements)
    source_ref[...] = jnp.where(active, right_ref[...], 0.0)
    relax_ref[...] = jnp.where(active, OMEGA / scale_ref[...], 0.0)
    kids, _, cdof = prolong_ref.shape
    lead_ref[rows:, :] = smooth_ref[...]
    for kid in range(kids):
        lead_ref[kid * cdof : (kid + 1) * cdof, :] = dot_t(csmooth_ref[...], prolong_ref[kid])
    lead = lead_ref[...]
    folded_ref[:, 0:rows] = dot(lead, elem_ref[...])
    for face in range(FACES):
        folded_ref[:, rows * (face + 1) : rows * (face + 2)] = dot(lead, faces_ref[face])
    local_blocks(start_ref, scale_ref, fscale_ref, nbr_ref, g_ref)
    change = dot(smooth_ref[...], source_ref[...]) - dot(folded_ref[rows:, :], g_ref[...])
    part_ref[...] = start_ref[...] + relax_ref[...] * change


def smoothed_kernel(
    flags_ref, part_ref, relax_ref, folded_ref, fscale_ref, nbr_ref, send_ref, p0, p1, p2, p3, smoothed_ref, *rest
):
    outs, g_ref = rest[:4], rest[4]
    rows, elements = part_ref.shape
    ghost_blocks(flags_ref, (p0, p1, p2, p3), rows, elements, fscale_ref, nbr_ref, g_ref)
    smoothed_ref[...] = part_ref[...] - relax_ref[...] * dot(folded_ref[rows:, rows:], g_ref[...])
    pack(flags_ref, send_ref[...], smoothed_ref, outs, rows, elements)


def second_local_kernel(
    flags_ref,
    counts_ref,
    smoothed_ref,
    source_ref,
    scale_ref,
    fscale_ref,
    nbr_ref,
    lead_ref,
    folded_ref,
    prolong_ref,
    slot_ref,
    cscale_ref,
    cfscale_ref,
    cnbr_ref,
    p0,
    p1,
    p2,
    p3,
    value_ref,
    spread_ref,
    prol_ref,
    place_ref,
    child_ref,
    weight_ref,
    table_ref,
    g_ref,
    *,
    mesh_shape,
    sent,
):
    rows, elements = smoothed_ref.shape
    wides, narrows = mesh_shape
    kids, _, cdof = prolong_ref.shape
    coarse = cscale_ref.shape[1]
    local_blocks(smoothed_ref, scale_ref, fscale_ref, nbr_ref, g_ref)
    value_ref[...] = dot(lead_ref[...], source_ref[...]) - dot(folded_ref[...], g_ref[...])

    for kid in range(kids):
        prol_ref[:, kid * cdof : (kid + 1) * cdof] = prolong_ref[kid]
    prol = prol_ref[...]
    for block in range(FACES + 1):
        cols = slice(rows * block, rows * (block + 1))
        spread_ref[:, cols] = dot(folded_ref[rows:, cols], prol)

    active = activity(counts_ref, elements)
    own = jnp.where(active, slot_ref[...], -1)
    halves = received(flags_ref, (p0, p1, p2, p3), rows)
    tiles = [rows8(own[:, c : c + LANES].astype(jnp.float32)) for c in range(0, elements, LANES)]
    tiles += [rows8(half[0:1]) for half in halves]
    line = lax.broadcasted_iota(jnp.int32, (SUB, LANES), 0)
    blank = jnp.zeros((SUB - FACES, LANES), jnp.int32)
    side = halves[0].shape[1] // 2
    for c in range(0, elements, LANES):
        cols = slice(c, c + LANES)
        entry = jnp.concatenate([nbr_ref[:, cols], blank], axis=0)
        slot = pick(tiles, jnp.maximum(entry, 0)).astype(jnp.int32)
        slot = jnp.where(line == FACES, rows8(own[:, cols]), slot)
        live = (slot >= 0) & (entry >= 0)
        slot = jnp.where(live, slot, 0)
        group = jnp.where(entry >= elements, 1 + (entry - elements) // side, 0)
        place_ref[:, cols] = group * coarse + slot // kids
        child_ref[:, cols] = slot % kids
        weight = jnp.concatenate([fscale_ref[:, cols], scale_ref[:, cols], scale_ref[:, cols]], axis=0)
        weight_ref[:, cols] = jnp.where(live, weight, 0.0)

    wide, narrow = flags_ref[AT_W], flags_ref[AT_N]
    me = wide * narrows + narrow
    owners = (
        lax.rem(wide + wides - 1, wides) * narrows + narrow,
        lax.rem(wide + 1, wides) * narrows + narrow,
        wide * narrows + lax.rem(narrow + narrows - 1, narrows),
        wide * narrows + lax.rem(narrow + 1, narrows),
    )
    entry = jnp.concatenate([cnbr_ref[...], jnp.zeros((SUB - FACES, coarse), jnp.int32)], axis=0)
    remote = entry - coarse
    direction = remote // sent
    offset = jnp.maximum(remote - direction * sent, 0)
    wanted = jnp.clip(jnp.where(direction == 1, side, jnp.where(direction == 3, side, 0)) + offset, 0, LANES - 1)
    pad = jnp.zeros((SUB, LANES - coarse), jnp.int32)
    wanted = jnp.concatenate([wanted, pad], axis=1) if coarse < LANES else wanted
    lists = [rows8(half[1:2]) for half in halves]
    first = lane_take(lists[0], wanted)[:, :coarse].astype(jnp.int32)
    second = lane_take(lists[1], wanted)[:, :coarse].astype(jnp.int32)
    there = jnp.where(direction < 2, first, second)
    owner = jnp.where(
        direction == 0,
        owners[0],
        jnp.where(direction == 1, owners[1], jnp.where(direction == 2, owners[2], owners[3])),
    )
    target = jnp.where(entry < coarse, me * coarse + entry, owner * coarse + there)
    ones = jnp.zeros((SUB - FACES, coarse), jnp.float32)
    cweight = jnp.concatenate([cfscale_ref[...] * (COARSE_OMEGA / cscale_ref[...]), ones], axis=0)
    table_ref[0:SUB, :] = jnp.where(entry >= 0, target, 0).astype(jnp.float32)
    table_ref[SUB:, :] = jnp.where(entry >= 0, cweight, 0.0)


def restrict_kernel(
    flags_ref,
    value_ref,
    smoothed_ref,
    relax_ref,
    folded_ref,
    fscale_ref,
    nbr_ref,
    slot_ref,
    cscale_ref,
    table_ref,
    p0,
    p1,
    p2,
    p3,
    base_ref,
    message_ref,
    g_ref,
    *,
    kids,
):
    rows, elements = smoothed_ref.shape
    coarse = cscale_ref.shape[1]
    ghost_blocks(flags_ref, (p0, p1, p2, p3), rows, elements, fscale_ref, nbr_ref, g_ref)
    value = value_ref[...] - dot(folded_ref[:, rows:], g_ref[...])
    base_ref[...] = smoothed_ref[...] + relax_ref[...] * value[rows:, :]
    slot = slot_ref[...]
    child = rows8(slot % kids)
    step = rows // kids
    summed = jnp.where(child == 0, value[0:step, :], 0.0)
    for kid in range(1, kids):
        summed = jnp.where(child == kid, value[kid * step : (kid + 1) * step, :], summed)
    member = lax.broadcasted_iota(jnp.int32, (coarse, elements), 0) == slot // kids
    first = dot_t(summed, member.astype(jnp.float32)) * (COARSE_OMEGA / cscale_ref[...])
    upper = jnp.concatenate([first, table_ref[0:SUB, :]], axis=1)
    lower = jnp.concatenate([table_ref[SUB:, :], jnp.zeros_like(first)], axis=1)
    for device in range(message_ref.shape[0]):
        message_ref[device, 0:SUB, :] = upper
        message_ref[device, SUB:, :] = lower


def neighbourhood(mesh_shape, reach):
    wides, narrows = mesh_shape
    seen, found = set(), []
    near = [(0, 0), (-1, 0), (1, 0), (0, -1), (0, 1)]
    found.extend(near)
    seen.update((w % wides, n % narrows) for w, n in near)
    counts = [1, len(found)]
    for distance in range(2, reach + 1):
        for w in range(-distance, distance + 1):
            for n in {distance - abs(w), abs(w) - distance}:
                key = (w % wides, n % narrows)
                if key not in seen:
                    seen.add(key)
                    found.append((w, n))
        counts.append(len(found))
    return found, counts


def paired(pieces):
    if len(pieces) % 2:
        pieces = pieces + [pieces[0]]
    return [jnp.concatenate(pieces[i : i + 2], axis=1) for i in range(0, len(pieces), 2)]


def finish_kernel(
    flags_ref,
    message_ref,
    base_ref,
    relax_ref,
    prol_ref,
    spread_ref,
    place_ref,
    child_ref,
    weight_ref,
    cblock_ref,
    csmooth_ref,
    cfaces_ref,
    field_ref,
    correction_ref,
    folded_ref,
    cg_ref,
    g_ref,
    *,
    mesh_shape,
    kids,
):
    rows, elements = base_ref.shape
    cdof, coarse = correction_ref.shape
    wides, narrows = mesh_shape
    offsets, counts = neighbourhood(mesh_shape, 3)
    parts = []
    for w, n in offsets:
        at_w = lax.rem(flags_ref[AT_W] + (w % wides), wides)
        at_n = lax.rem(flags_ref[AT_N] + (n % narrows), narrows)
        parts.append(at_w * narrows + at_n)
    csmooth = csmooth_ref[...]
    own = COARSE_OMEGA * dot(csmooth, cblock_ref[...])
    for face in range(FACES):
        folded_ref[:, face * cdof : (face + 1) * cdof] = dot(csmooth, cfaces_ref[face])
    folded = folded_ref[...]

    blocks = wides * narrows
    lane = lax.broadcasted_iota(jnp.int32, (SUB, LANES), 1)
    ranks = []
    for base in range(0, blocks, LANES):
        rank = jnp.zeros((SUB, LANES), jnp.int32)
        for position, part in reversed(list(enumerate(parts))):
            rank = jnp.where(lane + base == part, position, rank)
        ranks.append(rank)

    uppers = [message_ref[part, 0:SUB, :] for part in parts]
    first = paired([upper[:, :coarse] for upper in uppers])
    current = first
    for sweep, count in ((1, counts[2]), (2, counts[1])):
        following = []
        targets = paired([uppers[i][:, coarse:] for i in range(count)])
        weights = paired([message_ref[parts[i], SUB:, :coarse] for i in range(count)])
        for t in range(len(targets)):
            target = targets[t].astype(jnp.int32)
            index = pick(ranks, target // coarse) * coarse + target % coarse
            for face in range(FACES):
                chosen = pick(current, rows8(index[face : face + 1]))
                cg_ref[face * cdof : (face + 1) * cdof, t * LANES : (t + 1) * LANES] = (
                    rows8(weights[t][face : face + 1]) * chosen
                )
        width = len(targets) * LANES
        pulled = dot(folded, cg_ref[:, :width])
        inner = dot(own, jnp.concatenate(current[: len(targets)], axis=1))
        for t in range(len(targets)):
            cols = slice(t * LANES, (t + 1) * LANES)
            following.append(current[t] + first[t] - inner[:, cols] - pulled[:, cols])
        current = following
    correction_ref[...] = current[0][:, :coarse]

    for c in range(0, elements, LANES):
        cols = slice(c, c + LANES)
        for row in range(FACES + 1):
            block = 0 if row == FACES else row + 1
            chosen = pick(current, rows8(place_ref[row : row + 1, cols]))
            child = rows8(child_ref[row : row + 1, cols])
            if row == FACES:
                live = rows8(jnp.where(weight_ref[row : row + 1, cols] > 0.0, 1.0, 0.0)) * chosen
                for kid in range(kids):
                    at = (FACES + 1) * rows + kid * cdof
                    g_ref[at : at + cdof, cols] = jnp.where(child == kid, live, 0.0)
            chosen = rows8(weight_ref[row : row + 1, cols]) * chosen
            for kid in range(kids):
                at = block * rows + kid * cdof
                g_ref[at : at + cdof, cols] = jnp.where(child == kid, chosen, 0.0)
    split = (FACES + 1) * rows
    change = dot(spread_ref[...], g_ref[0:split, :])
    delta = dot(prol_ref[...], g_ref[split:, :])
    field_ref[...] = base_ref[...] + delta - relax_ref[...] * change


def swap_routes(size):
    if size % 2:
        return [[(i, (i + 1) % size) for i in range(size)], [(i, (i - 1) % size) for i in range(size)]]
    return [
        [(i, i + 1 if i % 2 == 0 else i - 1) for i in range(size)],
        [(i, (i - 1 if i % 2 == 0 else i + 1) % size) for i in range(size)],
    ]


def exchange(packets):
    moved = []
    for base, axis in ((0, "wide"), (2, "narrow")):
        for half, route in enumerate(swap_routes(lax.axis_size(axis))):
            moved.append(lax.ppermute(packets[base + half], axis, route))
    return moved


def position_flags():
    flags = []
    for axis in ("wide", "narrow"):
        at = lax.axis_index(axis)
        if lax.axis_size(axis) % 2:
            flags += [jnp.int32(0), jnp.int32(0)]
        else:
            flags += [at % 2, 1 - at % 2]
    return jnp.stack(flags + [lax.axis_index("wide"), lax.axis_index("narrow")]).astype(jnp.int32)


SMEM = pl.BlockSpec(memory_space=pltpu.SMEM)
VMEM = pl.BlockSpec(memory_space=pltpu.VMEM)


def call(kernel, name, scalars, arrays, shapes, scratch=(), flops=0):
    outs = [jax.ShapeDtypeStruct(shape, dtype) for shape, dtype in shapes]
    moved = sum(x.size * 4 for x in arrays)
    return pl.pallas_call(
        kernel,
        name=name,
        out_shape=outs,
        in_specs=[SMEM] * len(scalars) + [VMEM] * len(arrays),
        out_specs=[VMEM] * len(outs),
        scratch_shapes=[pltpu.VMEM(shape, jnp.float32) for shape in scratch],
        cost_estimate=pl.CostEstimate(flops=flops, bytes_accessed=moved, transcendentals=0),
    )(*scalars, *arrays)


def body(
    start_field,
    right_side,
    element_scale,
    face_scale,
    face_nbr,
    send_list,
    counts,
    coarse_slot,
    elem_block,
    smooth_block,
    face_blocks,
    prolong,
    coarse_scale,
    coarse_face_scale,
    coarse_nbr,
    coarse_send,
    coarse_block,
    coarse_smooth,
    coarse_faces,
):
    rows, elements = start_field.shape
    kids, _, cdof = prolong.shape
    coarse = coarse_scale.shape[0]
    sent = send_list.shape[1]
    mesh_shape = (lax.axis_size("wide"), lax.axis_size("narrow"))
    devices = mesh_shape[0] * mesh_shape[1]
    f32, i32 = jnp.float32, jnp.int32
    scale = element_scale.reshape(1, elements)
    slot = coarse_slot.reshape(1, elements)
    cscale = coarse_scale.reshape(1, coarse)
    flags = position_flags()
    blocks = (FACES + 1) * rows

    start, *packets = call(
        start_kernel,
        "start",
        (flags, counts),
        (start_field, slot, send_list, coarse_send),
        [((rows, elements), f32)] + [((rows + SUB, sent), f32)] * 4,
    )
    first_ghosts = exchange(packets)
    part, folded, lead, relax, source = call(
        first_local_kernel,
        "first_local",
        (counts,),
        (
            start,
            right_side,
            scale,
            face_scale,
            face_nbr,
            elem_block,
            smooth_block,
            face_blocks,
            prolong,
            coarse_smooth,
        ),
        [
            ((rows, elements), f32),
            ((2 * rows, blocks), f32),
            ((2 * rows, rows), f32),
            ((1, elements), f32),
            ((rows, elements), f32),
        ],
        [(blocks, elements)],
        flops=2 * blocks * rows * elements,
    )
    smoothed, *packets = call(
        smoothed_kernel,
        "smoothed",
        (flags,),
        (part, relax, folded, face_scale, face_nbr, send_list, *first_ghosts),
        [((rows, elements), f32)] + [((rows, sent), f32)] * 4,
        [(blocks - rows, elements)],
        flops=2 * blocks * rows * elements,
    )
    second_ghosts = exchange(packets)
    value, spread, prol, place, child, weight, table = call(
        functools.partial(second_local_kernel, mesh_shape=mesh_shape, sent=coarse_send.shape[1]),
        "second_local",
        (flags, counts),
        (
            smoothed,
            source,
            scale,
            face_scale,
            face_nbr,
            lead,
            folded,
            prolong,
            slot,
            cscale,
            coarse_face_scale,
            coarse_nbr,
            *first_ghosts,
        ),
        [
            ((2 * rows, elements), f32),
            ((rows, blocks), f32),
            ((rows, kids * cdof), f32),
            ((SUB, elements), i32),
            ((SUB, elements), i32),
            ((SUB, elements), f32),
            ((2 * SUB, coarse), f32),
        ],
        [(blocks, elements)],
        flops=4 * blocks * rows * elements,
    )
    base, message = call(
        functools.partial(restrict_kernel, kids=kids),
        "restrict",
        (flags,),
        (value, smoothed, relax, folded, face_scale, face_nbr, slot, cscale, table, *second_ghosts),
        [((rows, elements), f32), ((devices, 2 * SUB, 2 * coarse), f32)],
        [(blocks - rows, elements)],
        flops=4 * blocks * rows * elements,
    )
    gathered = lax.all_to_all(message, ("wide", "narrow"), 0, 0)
    needed = -(-neighbourhood(mesh_shape, 3)[1][2] // 2) * 2 * coarse
    return tuple(
        call(
            functools.partial(finish_kernel, mesh_shape=mesh_shape, kids=kids),
            "finish",
            (flags,),
            (
                gathered,
                base,
                relax,
                prol,
                spread,
                place,
                child,
                weight,
                coarse_block,
                coarse_smooth,
                coarse_faces,
            ),
            [((rows, elements), f32), ((cdof, coarse), f32)],
            [(cdof, FACES * cdof), (FACES * cdof, needed), (blocks + rows, elements)],
            flops=2 * blocks * rows * elements,
        )
    )


def solution(mesh):
    both = ("wide", "narrow")
    return jax.shard_map(
        body,
        mesh=mesh,
        in_specs=(
            P(None, both),
            P(None, both),
            P(both),
            P(None, both),
            P(None, both),
            P(None, both),
            P(both),
            P(both),
            P(),
            P(),
            P(),
            P(),
            P(both),
            P(None, both),
            P(None, both),
            P(None, both),
            P(),
            P(),
            P(),
        ),
        out_specs=(P(None, both), P(None, both)),
        check_vma=False,
    )
```

```python
import functools

import jax
import jax.numpy as jnp
from jax import lax
from jax.experimental import pallas as pl
from jax.experimental.pallas import tpu as pltpu
from jax.sharding import PartitionSpec as P

OMEGA = 0.7
COARSE_OMEGA = 0.6
HIGH = lax.Precision.HIGHEST
LANES = 128
SUB = 8
FACES = 6
GRANT = 16 * 1024 * 1024


def dot(left, right):
    return jnp.dot(left, right, preferred_element_type=jnp.float32, precision=HIGH)


def dot_t(left, right):
    return lax.dot_general(
        left, right, (((1,), (1,)), ((), ())), preferred_element_type=jnp.float32, precision=HIGH
    )


def lane_take(tile, index):
    return jnp.take_along_axis(tile, index, axis=1, mode="promise_in_bounds")


def pick(tiles, index):
    low = index & (LANES - 1)
    high = index >> 7
    found = lane_take(tiles[0], low)
    for place in range(1, len(tiles)):
        found = jnp.where(high == place, lane_take(tiles[place], low), found)
    return found


def rows8(row):
    return jnp.broadcast_to(row, (SUB, row.shape[1]))


def swapped(axis, one, other):
    if lax.axis_size(axis) % 2:
        return one, other
    odd = lax.rem(lax.axis_index(axis), 2) != 0
    return jnp.where(odd, other, one), jnp.where(odd, one, other)


def activity(counts_ref, elements):
    lane = lax.broadcasted_iota(jnp.int32, (1, elements), 1)
    return lane < counts_ref[0]


def ordered_sends(send):
    out = []
    for base, axis in ((0, "wide"), (2, "narrow")):
        out.extend(swapped(axis, send[base : base + 1], send[base + 1 : base + 2]))
    return out


def store_packets(outs, halves, row):
    size = outs[0].shape[1]
    for half, tile in enumerate(halves):
        outs[2 * half][row : row + SUB, :] = tile[:, :size]
        outs[2 * half + 1][row : row + SUB, :] = tile[:, size : 2 * size]


def pack(send, source_ref, outs, rows, elements):
    order = ordered_sends(send)
    index = [rows8(jnp.concatenate(order[:2], axis=1)), rows8(jnp.concatenate(order[2:], axis=1))]
    for row in range(0, rows, SUB):
        tiles = [source_ref[row : row + SUB, c : c + LANES] for c in range(0, elements, LANES)]
        store_packets(outs, [pick(tiles, which) for which in index], row)
    return index


def received(packets, row):
    tiles = []
    for base, axis in ((0, "wide"), (2, "narrow")):
        first = packets[base][row : row + SUB, :]
        second = packets[base + 1][row : row + SUB, :]
        if lax.axis_size(axis) % 2 == 0:
            first, second = swapped(axis, second, first)
        tiles.append(jnp.concatenate([first, second], axis=1))
    return tiles


def start_kernel(counts_ref, *refs, carried):
    given, refs = refs[: carried + 3], refs[carried + 3 :]
    masked_ref, outs, kept = refs[0], refs[1:5], refs[5 : 5 + carried]
    start_ref, send_ref, csend_ref, sems = refs[5 + carried :]
    slot_ref = kept[0]
    held = (start_ref, send_ref, csend_ref, *kept)
    copies = [pltpu.make_async_copy(here, there, sems.at[i]) for i, (here, there) in enumerate(zip(given, held))]
    for copy in copies:
        copy.start()
    for copy in copies[:4]:
        copy.wait()
    rows, elements = start_ref.shape
    active = activity(counts_ref, elements)
    masked_ref[...] = jnp.where(active, start_ref[...], 0.0)
    index = pack(send_ref[...], masked_ref, outs, rows, elements)
    slots = rows8(jnp.where(active, slot_ref[...], -1).astype(jnp.float32))
    tiles = [slots[:, c : c + LANES] for c in range(0, elements, LANES)]
    csend = csend_ref[...].astype(jnp.float32)
    blank = jnp.zeros((1, LANES // 2 - csend.shape[1]), jnp.float32)
    order = ordered_sends(csend)
    line = lax.broadcasted_iota(jnp.int32, (SUB, LANES), 0)
    halves = []
    for half in range(2):
        coarse = jnp.concatenate([order[2 * half], blank, order[2 * half + 1], blank], axis=1)
        halves.append(jnp.where(line == 0, pick(tiles, index[half]), rows8(coarse)))
    store_packets(outs, halves, rows)
    for copy in copies[4:]:
        copy.wait()


def local_blocks(current_ref, scale_ref, fscale_ref, nbr_ref, g_ref):
    rows, elements = current_ref.shape
    for c in range(0, elements, LANES):
        cols = slice(c, c + LANES)
        g_ref[0:rows, cols] = current_ref[:, cols] * scale_ref[:, cols]
    for face in range(FACES):
        for c in range(0, elements, LANES):
            cols = slice(c, c + LANES)
            entry = nbr_ref[face : face + 1, cols]
            here = (entry >= 0) & (entry < elements)
            weight = rows8(jnp.where(here, fscale_ref[face : face + 1, cols], 0.0))
            index = rows8(jnp.where(here, entry, 0))
            for row in range(0, rows, SUB):
                tiles = [current_ref[row : row + SUB, k : k + LANES] for k in range(0, elements, LANES)]
                at = rows * (face + 1) + row
                g_ref[at : at + SUB, cols] = weight * pick(tiles, index)


def ghost_blocks(packets, rows, elements, fscale_ref, nbr_ref, g_ref):
    halves = [received(packets, row) for row in range(0, rows, SUB)]
    for face in range(FACES):
        for c in range(0, elements, LANES):
            cols = slice(c, c + LANES)
            entry = nbr_ref[face : face + 1, cols]
            there = entry >= elements
            weight = rows8(jnp.where(there, fscale_ref[face : face + 1, cols], 0.0))
            index = rows8(jnp.where(there, entry - elements, 0))
            for row in range(0, rows, SUB):
                at = rows * face + row
                g_ref[at : at + SUB, cols] = weight * pick(halves[row // SUB], index)


def first_local_kernel(
    counts_ref,
    start_ref,
    right_ref,
    scale_ref,
    fscale_ref,
    nbr_ref,
    elem_ref,
    smooth_ref,
    faces_ref,
    prolong_ref,
    csmooth_ref,
    part_ref,
    folded_ref,
    lead_ref,
    relax_ref,
    source_ref,
    g_ref,
):
    rows, elements = start_ref.shape
    active = activity(counts_ref, elements)
    source_ref[...] = jnp.where(active, right_ref[...], 0.0)
    relax_ref[...] = jnp.where(active, OMEGA / scale_ref[...], 0.0)
    cdof = csmooth_ref.shape[0]
    lead_ref[rows:, :] = smooth_ref[...]
    for at in range(0, prolong_ref.shape[0], cdof):
        lead_ref[at : at + cdof, :] = dot(csmooth_ref[...], prolong_ref[at : at + cdof, :])
    lead = lead_ref[...]
    folded_ref[:, 0:rows] = dot(lead, elem_ref[...])
    for face in range(FACES):
        folded_ref[:, rows * (face + 1) : rows * (face + 2)] = dot(lead, faces_ref[face])
    local_blocks(start_ref, scale_ref, fscale_ref, nbr_ref, g_ref)
    change = dot(smooth_ref[...], source_ref[...]) - dot(folded_ref[rows:, :], g_ref[...])
    part_ref[...] = start_ref[...] + relax_ref[...] * change


def smoothed_kernel(
    part_ref, relax_ref, folded_ref, fscale_ref, nbr_ref, send_ref, p0, p1, p2, p3, smoothed_ref, *rest
):
    outs, g_ref = rest[:4], rest[4]
    rows, elements = part_ref.shape
    ghost_blocks((p0, p1, p2, p3), rows, elements, fscale_ref, nbr_ref, g_ref)
    smoothed_ref[...] = part_ref[...] - relax_ref[...] * dot(folded_ref[rows:, rows:], g_ref[...])
    pack(send_ref[...], smoothed_ref, outs, rows, elements)


def second_local_kernel(
    counts_ref,
    smoothed_ref,
    source_ref,
    scale_ref,
    fscale_ref,
    nbr_ref,
    lead_ref,
    folded_ref,
    prolong_ref,
    slot_ref,
    cscale_ref,
    cfscale_ref,
    cnbr_ref,
    p0,
    p1,
    p2,
    p3,
    value_ref,
    spread_ref,
    prol_ref,
    place_ref,
    child_ref,
    weight_ref,
    table_ref,
    g_ref,
    *,
    mesh_shape,
    sent,
    kids,
):
    rows, elements = smoothed_ref.shape
    wides, narrows = mesh_shape
    coarse = cscale_ref.shape[1]
    local_blocks(smoothed_ref, scale_ref, fscale_ref, nbr_ref, g_ref)
    value_ref[...] = dot(lead_ref[...], source_ref[...]) - dot(folded_ref[...], g_ref[...])

    prol_ref[...] = prolong_ref[...].T
    prol = prol_ref[...]
    for block in range(FACES + 1):
        cols = slice(rows * block, rows * (block + 1))
        spread_ref[:, cols] = dot(folded_ref[rows:, cols], prol)

    active = activity(counts_ref, elements)
    own = jnp.where(active, slot_ref[...], -1)
    halves = received((p0, p1, p2, p3), rows)
    tiles = [rows8(own[:, c : c + LANES].astype(jnp.float32)) for c in range(0, elements, LANES)]
    tiles += [rows8(half[0:1]) for half in halves]
    line = lax.broadcasted_iota(jnp.int32, (SUB, LANES), 0)
    blank = jnp.zeros((SUB - FACES, LANES), jnp.int32)
    side = halves[0].shape[1] // 2
    for c in range(0, elements, LANES):
        cols = slice(c, c + LANES)
        entry = jnp.concatenate([nbr_ref[:, cols], blank], axis=0)
        slot = pick(tiles, jnp.maximum(entry, 0)).astype(jnp.int32)
        slot = jnp.where(line == FACES, rows8(own[:, cols]), slot)
        live = (slot >= 0) & (entry >= 0)
        slot = jnp.where(live, slot, 0)
        group = jnp.where(entry >= elements, 1 + (entry - elements) // side, 0)
        place_ref[:, cols] = group * coarse + slot // kids
        child_ref[:, cols] = slot % kids
        weight = jnp.concatenate([fscale_ref[:, cols], scale_ref[:, cols], scale_ref[:, cols]], axis=0)
        weight_ref[:, cols] = jnp.where(live, weight, 0.0)

    wide, narrow = lax.axis_index("wide"), lax.axis_index("narrow")
    me = wide * narrows + narrow
    owners = (
        lax.rem(wide + wides - 1, wides) * narrows + narrow,
        lax.rem(wide + 1, wides) * narrows + narrow,
        wide * narrows + lax.rem(narrow + narrows - 1, narrows),
        wide * narrows + lax.rem(narrow + 1, narrows),
    )
    entry = jnp.concatenate([cnbr_ref[...], jnp.zeros((SUB - FACES, coarse), jnp.int32)], axis=0)
    remote = entry - coarse
    direction = remote // sent
    offset = jnp.maximum(remote - direction * sent, 0)
    wanted = jnp.clip(jnp.where(direction == 1, side, jnp.where(direction == 3, side, 0)) + offset, 0, LANES - 1)
    pad = jnp.zeros((SUB, LANES - coarse), jnp.int32)
    wanted = jnp.concatenate([wanted, pad], axis=1) if coarse < LANES else wanted
    lists = [rows8(half[1:2]) for half in halves]
    first = lane_take(lists[0], wanted)[:, :coarse].astype(jnp.int32)
    second = lane_take(lists[1], wanted)[:, :coarse].astype(jnp.int32)
    there = jnp.where(direction < 2, first, second)
    owner = jnp.where(
        direction == 0,
        owners[0],
        jnp.where(direction == 1, owners[1], jnp.where(direction == 2, owners[2], owners[3])),
    )
    target = jnp.where(entry < coarse, me * coarse + entry, owner * coarse + there)
    ones = jnp.zeros((SUB - FACES, coarse), jnp.float32)
    cweight = jnp.concatenate([cfscale_ref[...] * (COARSE_OMEGA / cscale_ref[...]), ones], axis=0)
    table_ref[0:SUB, :] = jnp.where(entry >= 0, target, 0).astype(jnp.float32)
    table_ref[SUB:, :] = jnp.where(entry >= 0, cweight, 0.0)


def restrict_kernel(
    value_ref,
    smoothed_ref,
    relax_ref,
    folded_ref,
    fscale_ref,
    nbr_ref,
    slot_ref,
    cscale_ref,
    table_ref,
    p0,
    p1,
    p2,
    p3,
    base_ref,
    message_ref,
    g_ref,
    *,
    kids,
):
    rows, elements = smoothed_ref.shape
    coarse = cscale_ref.shape[1]
    ghost_blocks((p0, p1, p2, p3), rows, elements, fscale_ref, nbr_ref, g_ref)
    value = value_ref[...] - dot(folded_ref[:, rows:], g_ref[...])
    base_ref[...] = smoothed_ref[...] + relax_ref[...] * value[rows:, :]
    slot = slot_ref[...]
    child = rows8(slot % kids)
    step = rows // kids
    summed = jnp.where(child == 0, value[0:step, :], 0.0)
    for kid in range(1, kids):
        summed = jnp.where(child == kid, value[kid * step : (kid + 1) * step, :], summed)
    member = lax.broadcasted_iota(jnp.int32, (coarse, elements), 0) == slot // kids
    first = dot_t(summed, member.astype(jnp.float32)) * (COARSE_OMEGA / cscale_ref[...])
    upper = jnp.concatenate([first, table_ref[0:SUB, :]], axis=1)
    lower = jnp.concatenate([table_ref[SUB:, :], jnp.zeros_like(first)], axis=1)
    for device in range(message_ref.shape[0]):
        message_ref[device, 0:SUB, :] = upper
        message_ref[device, SUB:, :] = lower


def neighbourhood(mesh_shape, reach):
    wides, narrows = mesh_shape
    seen, found = set(), []
    near = [(0, 0), (-1, 0), (1, 0), (0, -1), (0, 1)]
    found.extend(near)
    seen.update((w % wides, n % narrows) for w, n in near)
    counts = [1, len(found)]
    for distance in range(2, reach + 1):
        for w in range(-distance, distance + 1):
            for n in {distance - abs(w), abs(w) - distance}:
                key = (w % wides, n % narrows)
                if key not in seen:
                    seen.add(key)
                    found.append((w, n))
        counts.append(len(found))
    return found, counts


def paired(pieces):
    if len(pieces) % 2:
        pieces = pieces + [pieces[0]]
    return [jnp.concatenate(pieces[i : i + 2], axis=1) for i in range(0, len(pieces), 2)]


def finish_kernel(
    message_ref,
    base_ref,
    relax_ref,
    prol_ref,
    spread_ref,
    place_ref,
    child_ref,
    weight_ref,
    cblock_ref,
    csmooth_ref,
    cfaces_ref,
    field_ref,
    correction_ref,
    folded_ref,
    cg_ref,
    g_ref,
    *,
    mesh_shape,
    kids,
):
    rows, elements = base_ref.shape
    cdof, coarse = correction_ref.shape
    wides, narrows = mesh_shape
    offsets, counts = neighbourhood(mesh_shape, 3)
    parts = []
    for w, n in offsets:
        at_w = lax.rem(lax.axis_index("wide") + (w % wides), wides)
        at_n = lax.rem(lax.axis_index("narrow") + (n % narrows), narrows)
        parts.append(at_w * narrows + at_n)
    csmooth = csmooth_ref[...]
    own = COARSE_OMEGA * dot(csmooth, cblock_ref[...])
    for face in range(FACES):
        folded_ref[:, face * cdof : (face + 1) * cdof] = dot(csmooth, cfaces_ref[face])
    folded = folded_ref[...]

    blocks = wides * narrows
    lane = lax.broadcasted_iota(jnp.int32, (SUB, LANES), 1)
    ranks = []
    for base in range(0, blocks, LANES):
        rank = jnp.zeros((SUB, LANES), jnp.int32)
        for position, part in reversed(list(enumerate(parts))):
            rank = jnp.where(lane + base == part, position, rank)
        ranks.append(rank)

    uppers = [message_ref[part, 0:SUB, :] for part in parts]
    first = paired([upper[:, :coarse] for upper in uppers])
    current = first
    for sweep, count in ((1, counts[2]), (2, counts[1])):
        following = []
        targets = paired([uppers[i][:, coarse:] for i in range(count)])
        weights = paired([message_ref[parts[i], SUB:, :coarse] for i in range(count)])
        for t in range(len(targets)):
            target = targets[t].astype(jnp.int32)
            index = pick(ranks, target // coarse) * coarse + target % coarse
            for face in range(FACES):
                chosen = pick(current, rows8(index[face : face + 1]))
                cg_ref[face * cdof : (face + 1) * cdof, t * LANES : (t + 1) * LANES] = (
                    rows8(weights[t][face : face + 1]) * chosen
                )
        width = len(targets) * LANES
        pulled = dot(folded, cg_ref[:, :width])
        inner = dot(own, jnp.concatenate(current[: len(targets)], axis=1))
        for t in range(len(targets)):
            cols = slice(t * LANES, (t + 1) * LANES)
            following.append(current[t] + first[t] - inner[:, cols] - pulled[:, cols])
        current = following
    correction_ref[...] = current[0][:, :coarse]

    for c in range(0, elements, LANES):
        cols = slice(c, c + LANES)
        for row in range(FACES + 1):
            block = 0 if row == FACES else row + 1
            chosen = pick(current, rows8(place_ref[row : row + 1, cols]))
            child = rows8(child_ref[row : row + 1, cols])
            if row == FACES:
                live = rows8(jnp.where(weight_ref[row : row + 1, cols] > 0.0, 1.0, 0.0)) * chosen
                for kid in range(kids):
                    at = (FACES + 1) * rows + kid * cdof
                    g_ref[at : at + cdof, cols] = jnp.where(child == kid, live, 0.0)
            chosen = rows8(weight_ref[row : row + 1, cols]) * chosen
            for kid in range(kids):
                at = block * rows + kid * cdof
                g_ref[at : at + cdof, cols] = jnp.where(child == kid, chosen, 0.0)
    split = (FACES + 1) * rows
    change = dot(spread_ref[...], g_ref[0:split, :])
    delta = dot(prol_ref[...], g_ref[split:, :])
    field_ref[...] = base_ref[...] + delta - relax_ref[...] * change


def swap_routes(size):
    if size % 2:
        return [[(i, (i + 1) % size) for i in range(size)], [(i, (i - 1) % size) for i in range(size)]]
    return [
        [(i, i + 1 if i % 2 == 0 else i - 1) for i in range(size)],
        [(i, (i - 1 if i % 2 == 0 else i + 1) % size) for i in range(size)],
    ]


def exchange(packets):
    moved = []
    for base, axis in ((0, "wide"), (2, "narrow")):
        for half, route in enumerate(swap_routes(lax.axis_size(axis))):
            moved.append(lax.ppermute(packets[base + half], axis, route))
    return moved


SMEM = pl.BlockSpec(memory_space=pltpu.SMEM)
VMEM = pl.BlockSpec(memory_space=pltpu.VMEM)
HBM = pl.BlockSpec(memory_space=pltpu.HBM)


def call(kernel, name, scalars, arrays, shapes, scratch=(), flops=0, space=VMEM):
    outs = [jax.ShapeDtypeStruct(shape, dtype) for shape, dtype in shapes]
    if space is HBM:
        arrays = [pltpu.with_memory_space_constraint(x, pltpu.HBM) for x in arrays]
    moved = sum(x.size * 4 for x in arrays)
    return pl.pallas_call(
        kernel,
        name=name,
        out_shape=outs,
        in_specs=[SMEM] * len(scalars) + [space] * len(arrays),
        out_specs=[VMEM] * len(outs),
        scratch_shapes=[pltpu.VMEM(x, jnp.float32) if isinstance(x, tuple) else x for x in scratch],
        compiler_params=pltpu.CompilerParams(vmem_limit_bytes=GRANT),
        cost_estimate=pl.CostEstimate(flops=flops, bytes_accessed=moved, transcendentals=0),
    )(*scalars, *arrays)


def body(
    start_field,
    right_side,
    element_scale,
    face_scale,
    face_nbr,
    send_list,
    counts,
    coarse_slot,
    elem_block,
    smooth_block,
    face_blocks,
    prolong,
    coarse_scale,
    coarse_face_scale,
    coarse_nbr,
    coarse_send,
    coarse_block,
    coarse_smooth,
    coarse_faces,
):
    rows, elements = start_field.shape
    kids, _, cdof = prolong.shape
    prolong = prolong.transpose(0, 2, 1).reshape(kids * cdof, rows)
    coarse = coarse_scale.shape[0]
    sent = send_list.shape[1]
    mesh_shape = (lax.axis_size("wide"), lax.axis_size("narrow"))
    devices = mesh_shape[0] * mesh_shape[1]
    f32, i32 = jnp.float32, jnp.int32
    scale = element_scale.reshape(1, elements)
    slot = coarse_slot.reshape(1, elements)
    cscale = coarse_scale.reshape(1, coarse)
    blocks = (FACES + 1) * rows

    kept = (
        slot,
        right_side,
        scale,
        face_scale,
        face_nbr,
        elem_block,
        smooth_block,
        face_blocks,
        prolong,
        cscale,
        coarse_face_scale,
        coarse_nbr,
        coarse_block,
        coarse_smooth,
        coarse_faces,
        send_list,
    )
    start, *brought = call(
        functools.partial(start_kernel, carried=len(kept)),
        "start",
        (counts,),
        (start_field, send_list, coarse_send, *kept),
        [((rows, elements), f32)] + [((rows + SUB, sent), f32)] * 4 + [(x.shape, x.dtype) for x in kept],
        [
            pltpu.VMEM(start_field.shape, f32),
            pltpu.VMEM(send_list.shape, i32),
            pltpu.VMEM(coarse_send.shape, i32),
            pltpu.SemaphoreType.DMA((len(kept) + 3,)),
        ],
        space=HBM,
    )
    packets = brought[:4]
    (
        slot,
        right_side,
        scale,
        face_scale,
        face_nbr,
        elem_block,
        smooth_block,
        face_blocks,
        prolong,
        cscale,
        coarse_face_scale,
        coarse_nbr,
        coarse_block,
        coarse_smooth,
        coarse_faces,
        send_list,
    ) = brought[4:]
    first_ghosts = exchange(packets)
    part, folded, lead, relax, source = call(
        first_local_kernel,
        "first_local",
        (counts,),
        (
            start,
            right_side,
            scale,
            face_scale,
            face_nbr,
            elem_block,
            smooth_block,
            face_blocks,
            prolong,
            coarse_smooth,
        ),
        [
            ((rows, elements), f32),
            ((2 * rows, blocks), f32),
            ((2 * rows, rows), f32),
            ((1, elements), f32),
            ((rows, elements), f32),
        ],
        [(blocks, elements)],
        flops=2 * blocks * rows * elements,
    )
    smoothed, *packets = call(
        smoothed_kernel,
        "smoothed",
        (),
        (part, relax, folded, face_scale, face_nbr, send_list, *first_ghosts),
        [((rows, elements), f32)] + [((rows, sent), f32)] * 4,
        [(blocks - rows, elements)],
        flops=2 * blocks * rows * elements,
    )
    second_ghosts = exchange(packets)
    value, spread, prol, place, child, weight, table = call(
        functools.partial(second_local_kernel, mesh_shape=mesh_shape, sent=coarse_send.shape[1], kids=kids),
        "second_local",
        (counts,),
        (
            smoothed,
            source,
            scale,
            face_scale,
            face_nbr,
            lead,
            folded,
            prolong,
            slot,
            cscale,
            coarse_face_scale,
            coarse_nbr,
            *first_ghosts,
        ),
        [
            ((2 * rows, elements), f32),
            ((rows, blocks), f32),
            ((rows, kids * cdof), f32),
            ((SUB, elements), i32),
            ((SUB, elements), i32),
            ((SUB, elements), f32),
            ((2 * SUB, coarse), f32),
        ],
        [(blocks, elements)],
        flops=4 * blocks * rows * elements,
    )
    base, message = call(
        functools.partial(restrict_kernel, kids=kids),
        "restrict",
        (),
        (value, smoothed, relax, folded, face_scale, face_nbr, slot, cscale, table, *second_ghosts),
        [((rows, elements), f32), ((devices, 2 * SUB, 2 * coarse), f32)],
        [(blocks - rows, elements)],
        flops=4 * blocks * rows * elements,
    )
    gathered = lax.all_to_all(message, ("wide", "narrow"), 0, 0)
    needed = -(-neighbourhood(mesh_shape, 3)[1][2] // 2) * 2 * coarse
    return tuple(
        call(
            functools.partial(finish_kernel, mesh_shape=mesh_shape, kids=kids),
            "finish",
            (),
            (
                gathered,
                base,
                relax,
                prol,
                spread,
                place,
                child,
                weight,
                coarse_block,
                coarse_smooth,
                coarse_faces,
            ),
            [((rows, elements), f32), ((cdof, coarse), f32)],
            [(cdof, FACES * cdof), (FACES * cdof, needed), (blocks + rows, elements)],
            flops=2 * blocks * rows * elements,
        )
    )


def solution(mesh):
    both = ("wide", "narrow")
    return jax.shard_map(
        body,
        mesh=mesh,
        in_specs=(
            P(None, both),
            P(None, both),
            P(both),
            P(None, both),
            P(None, both),
            P(None, both),
            P(both),
            P(both),
            P(),
            P(),
            P(),
            P(),
            P(both),
            P(None, both),
            P(None, both),
            P(None, both),
            P(),
            P(),
            P(),
        ),
        out_specs=(P(None, both), P(None, both)),
        check_vma=False,
    )
```

```python
import functools

import jax
import jax.numpy as jnp
from jax import lax
from jax.experimental import pallas as pl
from jax.experimental.pallas import tpu as pltpu
from jax.sharding import PartitionSpec as P


OMEGA = 0.7
COARSE_OMEGA = 0.6
HIGH = lax.Precision.HIGHEST
LANES = 128
SUB = 8
FACES = 6
GRANT = 16 * 1024 * 1024


def dot(left, right):
    return jnp.dot(left, right, preferred_element_type=jnp.float32, precision=HIGH)


def dot_t(left, right):
    return lax.dot_general(
        left, right, (((1,), (1,)), ((), ())), preferred_element_type=jnp.float32, precision=HIGH
    )


def lane_take(tile, index):
    return jnp.take_along_axis(tile, index, axis=1, mode="promise_in_bounds")


def pick(tiles, index):
    low = index & (LANES - 1)
    high = index >> 7
    found = lane_take(tiles[0], low)
    for place in range(1, len(tiles)):
        found = jnp.where(high == place, lane_take(tiles[place], low), found)
    return found


def rows8(row):
    return jnp.broadcast_to(row, (SUB, row.shape[1]))


def swapped(axis, one, other):
    if lax.axis_size(axis) % 2:
        return one, other
    odd = lax.rem(lax.axis_index(axis), 2) != 0
    return jnp.where(odd, other, one), jnp.where(odd, one, other)


def activity(counts_ref, elements):
    lane = lax.broadcasted_iota(jnp.int32, (1, elements), 1)
    return lane < counts_ref[0]


def ordered_sends(send):
    out = []
    for base, axis in ((0, "wide"), (2, "narrow")):
        out.extend(swapped(axis, send[base : base + 1], send[base + 1 : base + 2]))
    return out


def store_packets(outs, halves, row):
    size = outs[0].shape[1]
    for half, tile in enumerate(halves):
        outs[2 * half][row : row + SUB, :] = tile[:, :size]
        outs[2 * half + 1][row : row + SUB, :] = tile[:, size : 2 * size]


def pack(send, source_ref, outs, rows, elements):
    order = ordered_sends(send)
    index = [rows8(jnp.concatenate(order[:2], axis=1)), rows8(jnp.concatenate(order[2:], axis=1))]
    for row in range(0, rows, SUB):
        tiles = [source_ref[row : row + SUB, c : c + LANES] for c in range(0, elements, LANES)]
        store_packets(outs, [pick(tiles, which) for which in index], row)
    return index


def received(packets, row):
    tiles = []
    for base, axis in ((0, "wide"), (2, "narrow")):
        first = packets[base][row : row + SUB, :]
        second = packets[base + 1][row : row + SUB, :]
        if lax.axis_size(axis) % 2 == 0:
            first, second = swapped(axis, second, first)
        tiles.append(jnp.concatenate([first, second], axis=1))
    return tiles


def start_kernel(counts_ref, *refs, carried):
    given, refs = refs[: carried + 3], refs[carried + 3 :]
    masked_ref, outs, kept = refs[0], refs[1:5], refs[5 : 5 + carried]
    start_ref, send_ref, csend_ref, sems = refs[5 + carried :]
    slot_ref = kept[0]
    held = (start_ref, send_ref, csend_ref, *kept)
    copies = [pltpu.make_async_copy(here, there, sems.at[i]) for i, (here, there) in enumerate(zip(given, held))]
    for copy in copies:
        copy.start()
    for copy in copies[:4]:
        copy.wait()
    rows, elements = start_ref.shape
    active = activity(counts_ref, elements)
    masked_ref[...] = jnp.where(active, start_ref[...], 0.0)
    index = pack(send_ref[...], masked_ref, outs, rows, elements)
    slots = rows8(jnp.where(active, slot_ref[...], -1).astype(jnp.float32))
    tiles = [slots[:, c : c + LANES] for c in range(0, elements, LANES)]
    csend = csend_ref[...].astype(jnp.float32)
    blank = jnp.zeros((1, LANES // 2 - csend.shape[1]), jnp.float32)
    order = ordered_sends(csend)
    line = lax.broadcasted_iota(jnp.int32, (SUB, LANES), 0)
    halves = []
    for half in range(2):
        coarse = jnp.concatenate([order[2 * half], blank, order[2 * half + 1], blank], axis=1)
        halves.append(jnp.where(line == 0, pick(tiles, index[half]), rows8(coarse)))
    store_packets(outs, halves, rows)
    for copy in copies[4:]:
        copy.wait()


def local_blocks(current_ref, scale_ref, fscale_ref, nbr_ref, g_ref):
    rows, elements = current_ref.shape
    for c in range(0, elements, LANES):
        cols = slice(c, c + LANES)
        g_ref[0:rows, cols] = current_ref[:, cols] * scale_ref[:, cols]
    for face in range(FACES):
        for c in range(0, elements, LANES):
            cols = slice(c, c + LANES)
            entry = nbr_ref[face : face + 1, cols]
            here = (entry >= 0) & (entry < elements)
            weight = rows8(jnp.where(here, fscale_ref[face : face + 1, cols], 0.0))
            index = rows8(jnp.where(here, entry, 0))
            for row in range(0, rows, SUB):
                tiles = [current_ref[row : row + SUB, k : k + LANES] for k in range(0, elements, LANES)]
                at = rows * (face + 1) + row
                g_ref[at : at + SUB, cols] = weight * pick(tiles, index)


def ghost_blocks(packets, rows, elements, fscale_ref, nbr_ref, g_ref):
    halves = [received(packets, row) for row in range(0, rows, SUB)]
    for face in range(FACES):
        for c in range(0, elements, LANES):
            cols = slice(c, c + LANES)
            entry = nbr_ref[face : face + 1, cols]
            there = entry >= elements
            weight = rows8(jnp.where(there, fscale_ref[face : face + 1, cols], 0.0))
            index = rows8(jnp.where(there, entry - elements, 0))
            for row in range(0, rows, SUB):
                at = rows * face + row
                g_ref[at : at + SUB, cols] = weight * pick(halves[row // SUB], index)


def first_local_kernel(
    counts_ref,
    start_ref,
    right_ref,
    scale_ref,
    fscale_ref,
    nbr_ref,
    elem_ref,
    smooth_ref,
    faces_ref,
    prolong_ref,
    csmooth_ref,
    part_ref,
    folded_ref,
    lead_ref,
    relax_ref,
    source_ref,
    g_ref,
):
    rows, elements = start_ref.shape
    active = activity(counts_ref, elements)
    source_ref[...] = jnp.where(active, right_ref[...], 0.0)
    relax_ref[...] = jnp.where(active, OMEGA / scale_ref[...], 0.0)
    cdof = csmooth_ref.shape[0]
    lead_ref[rows:, :] = smooth_ref[...]
    for at in range(0, prolong_ref.shape[0], cdof):
        lead_ref[at : at + cdof, :] = dot(csmooth_ref[...], prolong_ref[at : at + cdof, :])
    lead = lead_ref[...]
    folded_ref[:, 0:rows] = dot(lead, elem_ref[...])
    for face in range(FACES):
        folded_ref[:, rows * (face + 1) : rows * (face + 2)] = dot(lead, faces_ref[face])
    local_blocks(start_ref, scale_ref, fscale_ref, nbr_ref, g_ref)
    change = dot(smooth_ref[...], source_ref[...]) - dot(folded_ref[rows:, :], g_ref[...])
    part_ref[...] = start_ref[...] + relax_ref[...] * change


def smoothed_kernel(
    part_ref, relax_ref, folded_ref, fscale_ref, nbr_ref, send_ref, p0, p1, p2, p3, smoothed_ref, *rest
):
    outs, g_ref = rest[:4], rest[4]
    rows, elements = part_ref.shape
    ghost_blocks((p0, p1, p2, p3), rows, elements, fscale_ref, nbr_ref, g_ref)
    smoothed_ref[...] = part_ref[...] - relax_ref[...] * dot(folded_ref[rows:, rows:], g_ref[...])
    pack(send_ref[...], smoothed_ref, outs, rows, elements)


def second_local_kernel(
    counts_ref,
    smoothed_ref,
    source_ref,
    scale_ref,
    fscale_ref,
    nbr_ref,
    lead_ref,
    folded_ref,
    prolong_ref,
    slot_ref,
    cscale_ref,
    cfscale_ref,
    cnbr_ref,
    p0,
    p1,
    p2,
    p3,
    value_ref,
    spread_ref,
    prol_ref,
    place_ref,
    child_ref,
    weight_ref,
    table_ref,
    g_ref,
    *,
    mesh_shape,
    sent,
    kids,
):
    rows, elements = smoothed_ref.shape
    wides, narrows = mesh_shape
    coarse = cscale_ref.shape[1]
    local_blocks(smoothed_ref, scale_ref, fscale_ref, nbr_ref, g_ref)
    value_ref[...] = dot(lead_ref[...], source_ref[...]) - dot(folded_ref[...], g_ref[...])

    prol_ref[...] = prolong_ref[...].T
    prol = prol_ref[...]
    for block in range(FACES + 1):
        cols = slice(rows * block, rows * (block + 1))
        spread_ref[:, cols] = dot(folded_ref[rows:, cols], prol)

    active = activity(counts_ref, elements)
    own = jnp.where(active, slot_ref[...], -1)
    halves = received((p0, p1, p2, p3), rows)
    tiles = [rows8(own[:, c : c + LANES].astype(jnp.float32)) for c in range(0, elements, LANES)]
    tiles += [rows8(half[0:1]) for half in halves]
    line = lax.broadcasted_iota(jnp.int32, (SUB, LANES), 0)
    blank = jnp.zeros((SUB - FACES, LANES), jnp.int32)
    side = halves[0].shape[1] // 2
    for c in range(0, elements, LANES):
        cols = slice(c, c + LANES)
        entry = jnp.concatenate([nbr_ref[:, cols], blank], axis=0)
        slot = pick(tiles, jnp.maximum(entry, 0)).astype(jnp.int32)
        slot = jnp.where(line == FACES, rows8(own[:, cols]), slot)
        live = (slot >= 0) & (entry >= 0)
        slot = jnp.where(live, slot, 0)
        group = jnp.where(entry >= elements, 1 + (entry - elements) // side, 0)
        place_ref[:, cols] = group * coarse + slot // kids
        child_ref[:, cols] = slot % kids
        weight = jnp.concatenate([fscale_ref[:, cols], scale_ref[:, cols], scale_ref[:, cols]], axis=0)
        weight_ref[:, cols] = jnp.where(live, weight, 0.0)

    wide, narrow = lax.axis_index("wide"), lax.axis_index("narrow")
    me = wide * narrows + narrow
    owners = (
        lax.rem(wide + wides - 1, wides) * narrows + narrow,
        lax.rem(wide + 1, wides) * narrows + narrow,
        wide * narrows + lax.rem(narrow + narrows - 1, narrows),
        wide * narrows + lax.rem(narrow + 1, narrows),
    )
    entry = jnp.concatenate([cnbr_ref[...], jnp.zeros((SUB - FACES, coarse), jnp.int32)], axis=0)
    remote = entry - coarse
    direction = remote // sent
    offset = jnp.maximum(remote - direction * sent, 0)
    wanted = jnp.clip(jnp.where(direction == 1, side, jnp.where(direction == 3, side, 0)) + offset, 0, LANES - 1)
    pad = jnp.zeros((SUB, LANES - coarse), jnp.int32)
    wanted = jnp.concatenate([wanted, pad], axis=1) if coarse < LANES else wanted
    lists = [rows8(half[1:2]) for half in halves]
    first = lane_take(lists[0], wanted)[:, :coarse].astype(jnp.int32)
    second = lane_take(lists[1], wanted)[:, :coarse].astype(jnp.int32)
    there = jnp.where(direction < 2, first, second)
    owner = jnp.where(
        direction == 0,
        owners[0],
        jnp.where(direction == 1, owners[1], jnp.where(direction == 2, owners[2], owners[3])),
    )
    target = jnp.where(entry < coarse, me * coarse + entry, owner * coarse + there)
    ones = jnp.zeros((SUB - FACES, coarse), jnp.float32)
    cweight = jnp.concatenate([cfscale_ref[...] * (COARSE_OMEGA / cscale_ref[...]), ones], axis=0)
    table_ref[0:SUB, :] = jnp.where(entry >= 0, target, 0).astype(jnp.float32)
    table_ref[SUB:, :] = jnp.where(entry >= 0, cweight, 0.0)


def restrict_kernel(
    value_ref,
    smoothed_ref,
    relax_ref,
    folded_ref,
    fscale_ref,
    nbr_ref,
    slot_ref,
    cscale_ref,
    table_ref,
    p0,
    p1,
    p2,
    p3,
    base_ref,
    message_ref,
    g_ref,
    *,
    kids,
):
    rows, elements = smoothed_ref.shape
    coarse = cscale_ref.shape[1]
    ghost_blocks((p0, p1, p2, p3), rows, elements, fscale_ref, nbr_ref, g_ref)
    value = value_ref[...] - dot(folded_ref[:, rows:], g_ref[...])
    base_ref[...] = smoothed_ref[...] + relax_ref[...] * value[rows:, :]
    slot = slot_ref[...]
    child = rows8(slot % kids)
    step = rows // kids
    summed = jnp.where(child == 0, value[0:step, :], 0.0)
    for kid in range(1, kids):
        summed = jnp.where(child == kid, value[kid * step : (kid + 1) * step, :], summed)
    member = lax.broadcasted_iota(jnp.int32, (coarse, elements), 0) == slot // kids
    first = dot_t(summed, member.astype(jnp.float32)) * (COARSE_OMEGA / cscale_ref[...])
    upper = jnp.concatenate([first, table_ref[0:SUB, :]], axis=1)
    lower = jnp.concatenate([table_ref[SUB:, :], jnp.zeros_like(first)], axis=1)
    for device in range(message_ref.shape[0]):
        message_ref[device, 0:SUB, :] = upper
        message_ref[device, SUB:, :] = lower


def neighbourhood(mesh_shape, reach):
    wides, narrows = mesh_shape
    seen, found = set(), []
    near = [(0, 0), (-1, 0), (1, 0), (0, -1), (0, 1)]
    found.extend(near)
    seen.update((w % wides, n % narrows) for w, n in near)
    counts = [1, len(found)]
    for distance in range(2, reach + 1):
        for w in range(-distance, distance + 1):
            for n in {distance - abs(w), abs(w) - distance}:
                key = (w % wides, n % narrows)
                if key not in seen:
                    seen.add(key)
                    found.append((w, n))
        counts.append(len(found))
    return found, counts


def paired(pieces):
    if len(pieces) % 2:
        pieces = pieces + [pieces[0]]
    return [jnp.concatenate(pieces[i : i + 2], axis=1) for i in range(0, len(pieces), 2)]


def finish_kernel(
    message_ref,
    base_ref,
    relax_ref,
    prol_ref,
    spread_ref,
    place_ref,
    child_ref,
    weight_ref,
    cblock_ref,
    csmooth_ref,
    cfaces_ref,
    field_ref,
    correction_ref,
    folded_ref,
    cg_ref,
    g_ref,
    *,
    mesh_shape,
    kids,
):
    rows, elements = base_ref.shape
    cdof, coarse = correction_ref.shape
    wides, narrows = mesh_shape
    offsets, counts = neighbourhood(mesh_shape, 3)
    parts = []
    for w, n in offsets:
        at_w = lax.rem(lax.axis_index("wide") + (w % wides), wides)
        at_n = lax.rem(lax.axis_index("narrow") + (n % narrows), narrows)
        parts.append(at_w * narrows + at_n)
    csmooth = csmooth_ref[...]
    own = COARSE_OMEGA * dot(csmooth, cblock_ref[...])
    for face in range(FACES):
        folded_ref[:, face * cdof : (face + 1) * cdof] = dot(csmooth, cfaces_ref[face])
    folded = folded_ref[...]

    blocks = wides * narrows
    lane = lax.broadcasted_iota(jnp.int32, (SUB, LANES), 1)
    ranks = []
    for base in range(0, blocks, LANES):
        rank = jnp.zeros((SUB, LANES), jnp.int32)
        for position, part in reversed(list(enumerate(parts))):
            rank = jnp.where(lane + base == part, position, rank)
        ranks.append(rank)

    uppers = [message_ref[part, 0:SUB, :] for part in parts]
    first = paired([upper[:, :coarse] for upper in uppers])
    current = first
    for count in (counts[2], counts[1]):
        following = []
        targets = paired([uppers[i][:, coarse:] for i in range(count)])
        weights = paired([message_ref[parts[i], SUB:, :coarse] for i in range(count)])
        for t in range(len(targets)):
            target = targets[t].astype(jnp.int32)
            index = pick(ranks, target // coarse) * coarse + target % coarse
            for face in range(FACES):
                chosen = pick(current, rows8(index[face : face + 1]))
                cg_ref[face * cdof : (face + 1) * cdof, t * LANES : (t + 1) * LANES] = (
                    rows8(weights[t][face : face + 1]) * chosen
                )
        width = len(targets) * LANES
        pulled = dot(folded, cg_ref[:, :width])
        inner = dot(own, jnp.concatenate(current[: len(targets)], axis=1))
        for t in range(len(targets)):
            cols = slice(t * LANES, (t + 1) * LANES)
            following.append(current[t] + first[t] - inner[:, cols] - pulled[:, cols])
        current = following
    correction_ref[...] = current[0][:, :coarse]

    for c in range(0, elements, LANES):
        cols = slice(c, c + LANES)
        for row in range(FACES + 1):
            block = 0 if row == FACES else row + 1
            chosen = pick(current, rows8(place_ref[row : row + 1, cols]))
            child = rows8(child_ref[row : row + 1, cols])
            if row == FACES:
                live = rows8(jnp.where(weight_ref[row : row + 1, cols] > 0.0, 1.0, 0.0)) * chosen
                for kid in range(kids):
                    at = (FACES + 1) * rows + kid * cdof
                    g_ref[at : at + cdof, cols] = jnp.where(child == kid, live, 0.0)
            chosen = rows8(weight_ref[row : row + 1, cols]) * chosen
            for kid in range(kids):
                at = block * rows + kid * cdof
                g_ref[at : at + cdof, cols] = jnp.where(child == kid, chosen, 0.0)
    split = (FACES + 1) * rows
    change = dot(spread_ref[...], g_ref[0:split, :])
    delta = dot(prol_ref[...], g_ref[split:, :])
    field_ref[...] = base_ref[...] + delta - relax_ref[...] * change


def swap_routes(size):
    if size % 2:
        return [[(i, (i + 1) % size) for i in range(size)], [(i, (i - 1) % size) for i in range(size)]]
    return [
        [(i, i + 1 if i % 2 == 0 else i - 1) for i in range(size)],
        [(i, (i - 1 if i % 2 == 0 else i + 1) % size) for i in range(size)],
    ]


def exchange(packets):
    moved = []
    for base, axis in ((0, "wide"), (2, "narrow")):
        for half, route in enumerate(swap_routes(lax.axis_size(axis))):
            moved.append(lax.ppermute(packets[base + half], axis, route))
    return moved


SMEM = pl.BlockSpec(memory_space=pltpu.SMEM)
VMEM = pl.BlockSpec(memory_space=pltpu.VMEM)
HBM = pl.BlockSpec(memory_space=pltpu.HBM)


def call(kernel, scalars, arrays, shapes, scratch=(), flops=0, space=VMEM):
    outs = [jax.ShapeDtypeStruct(shape, dtype) for shape, dtype in shapes]
    if space is HBM:
        arrays = [pltpu.with_memory_space_constraint(x, pltpu.HBM) for x in arrays]
    moved = sum(x.size * 4 for x in arrays)
    return pl.pallas_call(
        kernel,
        out_shape=outs,
        in_specs=[SMEM] * len(scalars) + [space] * len(arrays),
        out_specs=[VMEM] * len(outs),
        scratch_shapes=[pltpu.VMEM(x, jnp.float32) if isinstance(x, tuple) else x for x in scratch],
        compiler_params=pltpu.CompilerParams(vmem_limit_bytes=GRANT),
        cost_estimate=pl.CostEstimate(flops=flops, bytes_accessed=moved, transcendentals=0),
    )(*scalars, *arrays)


def body(
    start_field,
    right_side,
    element_scale,
    face_scale,
    face_nbr,
    send_list,
    counts,
    coarse_slot,
    elem_block,
    smooth_block,
    face_blocks,
    prolong,
    coarse_scale,
    coarse_face_scale,
    coarse_nbr,
    coarse_send,
    coarse_block,
    coarse_smooth,
    coarse_faces,
):
    rows, elements = start_field.shape
    kids, _, cdof = prolong.shape
    prolong = prolong.transpose(0, 2, 1).reshape(kids * cdof, rows)
    coarse = coarse_scale.shape[0]
    sent = send_list.shape[1]
    mesh_shape = (lax.axis_size("wide"), lax.axis_size("narrow"))
    devices = mesh_shape[0] * mesh_shape[1]
    f32, i32 = jnp.float32, jnp.int32
    scale = element_scale.reshape(1, elements)
    slot = coarse_slot.reshape(1, elements)
    cscale = coarse_scale.reshape(1, coarse)
    blocks = (FACES + 1) * rows

    kept = (
        slot,
        right_side,
        scale,
        face_scale,
        face_nbr,
        elem_block,
        smooth_block,
        face_blocks,
        prolong,
        cscale,
        coarse_face_scale,
        coarse_nbr,
        coarse_block,
        coarse_smooth,
        coarse_faces,
        send_list,
    )
    start, *brought = call(
        functools.partial(start_kernel, carried=len(kept)),
        (counts,),
        (start_field, send_list, coarse_send, *kept),
        [((rows, elements), f32)] + [((rows + SUB, sent), f32)] * 4 + [(x.shape, x.dtype) for x in kept],
        [
            pltpu.VMEM(start_field.shape, f32),
            pltpu.VMEM(send_list.shape, i32),
            pltpu.VMEM(coarse_send.shape, i32),
            pltpu.SemaphoreType.DMA((len(kept) + 3,)),
        ],
        space=HBM,
    )
    packets = brought[:4]
    (
        slot,
        right_side,
        scale,
        face_scale,
        face_nbr,
        elem_block,
        smooth_block,
        face_blocks,
        prolong,
        cscale,
        coarse_face_scale,
        coarse_nbr,
        coarse_block,
        coarse_smooth,
        coarse_faces,
        send_list,
    ) = brought[4:]
    first_ghosts = exchange(packets)
    part, folded, lead, relax, source = call(
        first_local_kernel,
        (counts,),
        (
            start,
            right_side,
            scale,
            face_scale,
            face_nbr,
            elem_block,
            smooth_block,
            face_blocks,
            prolong,
            coarse_smooth,
        ),
        [
            ((rows, elements), f32),
            ((2 * rows, blocks), f32),
            ((2 * rows, rows), f32),
            ((1, elements), f32),
            ((rows, elements), f32),
        ],
        [(blocks, elements)],
        flops=2 * blocks * rows * elements,
    )
    smoothed, *packets = call(
        smoothed_kernel,
        (),
        (part, relax, folded, face_scale, face_nbr, send_list, *first_ghosts),
        [((rows, elements), f32)] + [((rows, sent), f32)] * 4,
        [(blocks - rows, elements)],
        flops=2 * blocks * rows * elements,
    )
    second_ghosts = exchange(packets)
    value, spread, prol, place, child, weight, table = call(
        functools.partial(second_local_kernel, mesh_shape=mesh_shape, sent=coarse_send.shape[1], kids=kids),
        (counts,),
        (
            smoothed,
            source,
            scale,
            face_scale,
            face_nbr,
            lead,
            folded,
            prolong,
            slot,
            cscale,
            coarse_face_scale,
            coarse_nbr,
            *first_ghosts,
        ),
        [
            ((2 * rows, elements), f32),
            ((rows, blocks), f32),
            ((rows, kids * cdof), f32),
            ((SUB, elements), i32),
            ((SUB, elements), i32),
            ((SUB, elements), f32),
            ((2 * SUB, coarse), f32),
        ],
        [(blocks, elements)],
        flops=4 * blocks * rows * elements,
    )
    base, message = call(
        functools.partial(restrict_kernel, kids=kids),
        (),
        (value, smoothed, relax, folded, face_scale, face_nbr, slot, cscale, table, *second_ghosts),
        [((rows, elements), f32), ((devices, 2 * SUB, 2 * coarse), f32)],
        [(blocks - rows, elements)],
        flops=4 * blocks * rows * elements,
    )
    gathered = lax.all_to_all(message, ("wide", "narrow"), 0, 0)
    needed = -(-neighbourhood(mesh_shape, 3)[1][2] // 2) * 2 * coarse
    return tuple(
        call(
            functools.partial(finish_kernel, mesh_shape=mesh_shape, kids=kids),
            (),
            (
                gathered,
                base,
                relax,
                prol,
                spread,
                place,
                child,
                weight,
                coarse_block,
                coarse_smooth,
                coarse_faces,
            ),
            [((rows, elements), f32), ((cdof, coarse), f32)],
            [(cdof, FACES * cdof), (FACES * cdof, needed), (blocks + rows, elements)],
            flops=2 * blocks * rows * elements,
        )
    )


def solution(mesh):
    both = ("wide", "narrow")

    return jax.shard_map(
        body,
        mesh=mesh,
        in_specs=(
            P(None, both),
            P(None, both),
            P(both),
            P(None, both),
            P(None, both),
            P(None, both),
            P(both),
            P(both),
            P(),
            P(),
            P(),
            P(),
            P(both),
            P(None, both),
            P(None, both),
            P(None, both),
            P(),
            P(),
            P(),
        ),
        out_specs=(P(None, both), P(None, both)),
        check_vma=False,
    )
```

```python
import functools

import jax
import jax.numpy as jnp
from jax import lax
from jax.experimental import pallas as pl
from jax.experimental.pallas import tpu as pltpu
from jax.sharding import PartitionSpec as P


OMEGA = 0.7
COARSE_OMEGA = 0.6
HIGH = lax.Precision.HIGH
HIGHEST = lax.Precision.HIGHEST
LANES = 128
SUB = 8
FACES = 6
GRANT = 16 * 1024 * 1024


def dot(left, right, precision=HIGH):
    return jnp.dot(left, right, preferred_element_type=jnp.float32, precision=precision)


def dot_t(left, right):
    return lax.dot_general(
        left, right, (((1,), (1,)), ((), ())), preferred_element_type=jnp.float32, precision=HIGH
    )


def lane_take(tile, index):
    return jnp.take_along_axis(tile, index, axis=1, mode="promise_in_bounds")


def pick(tiles, index):
    low = index & (LANES - 1)
    high = index >> 7
    found = lane_take(tiles[0], low)
    for place in range(1, len(tiles)):
        found = jnp.where(high == place, lane_take(tiles[place], low), found)
    return found


def rows8(row):
    return jnp.broadcast_to(row, (SUB, row.shape[1]))


def swapped(axis, one, other):
    if lax.axis_size(axis) % 2:
        return one, other
    odd = lax.rem(lax.axis_index(axis), 2) != 0
    return jnp.where(odd, other, one), jnp.where(odd, one, other)


def activity(counts_ref, elements):
    lane = lax.broadcasted_iota(jnp.int32, (1, elements), 1)
    return lane < counts_ref[0]


def ordered_sends(send):
    out = []
    for base, axis in ((0, "wide"), (2, "narrow")):
        out.extend(swapped(axis, send[base : base + 1], send[base + 1 : base + 2]))
    return out


def store_packets(outs, halves, row):
    size = outs[0].shape[1]
    for half, tile in enumerate(halves):
        outs[2 * half][row : row + SUB, :] = tile[:, :size]
        outs[2 * half + 1][row : row + SUB, :] = tile[:, size : 2 * size]


def pack(send, source_ref, outs, rows, elements):
    order = ordered_sends(send)
    index = [rows8(jnp.concatenate(order[:2], axis=1)), rows8(jnp.concatenate(order[2:], axis=1))]
    for row in range(0, rows, SUB):
        tiles = [source_ref[row : row + SUB, c : c + LANES] for c in range(0, elements, LANES)]
        store_packets(outs, [pick(tiles, which) for which in index], row)
    return index


def in_order(axis, first, second):
    if lax.axis_size(axis) % 2:
        return first, second
    return swapped(axis, second, first)


def received(packets, row):
    tiles = []
    for base, axis in ((0, "wide"), (2, "narrow")):
        pair = [packet[row : row + SUB, :] for packet in packets[base : base + 2]]
        tiles.append(jnp.concatenate(in_order(axis, *pair), axis=1))
    return tiles


def start_kernel(counts_ref, *refs, carried):
    given, refs = refs[: carried + 2], refs[carried + 2 :]
    masked_ref, outs, kept = refs[0], refs[1:5], refs[5 : 5 + carried]
    start_ref, send_ref, sems = refs[5 + carried :]
    slot_ref, cnbr_ref, csend_ref = kept[:3]
    held = (start_ref, send_ref, *kept)
    copies = [pltpu.make_async_copy(here, there, sems.at[i]) for i, (here, there) in enumerate(zip(given, held))]
    for copy in copies:
        copy.start()
    for copy in copies[:5]:
        copy.wait()
    rows, elements = start_ref.shape
    active = activity(counts_ref, elements)
    masked_ref[...] = jnp.where(active, start_ref[...], 0.0)
    index = pack(send_ref[...], masked_ref, outs, rows, elements)
    slots = rows8(jnp.where(active, slot_ref[...], -1).astype(jnp.float32))
    tiles = [slots[:, c : c + LANES] for c in range(0, elements, LANES)]
    csend = csend_ref[...].astype(jnp.float32)
    blank = jnp.zeros((1, LANES // 2 - csend.shape[1]), jnp.float32)
    order = ordered_sends(csend)
    table = cnbr_ref[...].astype(jnp.float32)
    table = jnp.concatenate([table, table], axis=1)
    halves = []
    for half in range(2):
        coarse = jnp.concatenate([order[2 * half], blank, order[2 * half + 1], blank], axis=1)
        halves.append(jnp.concatenate([pick(tiles, index[half])[0:1], coarse, table], axis=0))
    store_packets(outs, halves, rows)
    for copy in copies[5:]:
        copy.wait()


def local_blocks(current_ref, scale_ref, fscale_ref, nbr_ref, g_ref):
    rows, elements = current_ref.shape
    for c in range(0, elements, LANES):
        cols = slice(c, c + LANES)
        g_ref[0:rows, cols] = current_ref[:, cols] * scale_ref[:, cols]
    for face in range(FACES):
        for c in range(0, elements, LANES):
            cols = slice(c, c + LANES)
            entry = nbr_ref[face : face + 1, cols]
            here = (entry >= 0) & (entry < elements)
            weight = rows8(jnp.where(here, fscale_ref[face : face + 1, cols], 0.0))
            index = rows8(jnp.where(here, entry, 0))
            for row in range(0, rows, SUB):
                tiles = [current_ref[row : row + SUB, k : k + LANES] for k in range(0, elements, LANES)]
                at = rows * (face + 1) + row
                g_ref[at : at + SUB, cols] = weight * pick(tiles, index)


def ghost_blocks(packets, rows, elements, fscale_ref, nbr_ref, g_ref):
    halves = [received(packets, row) for row in range(0, rows, SUB)]
    for face in range(FACES):
        for c in range(0, elements, LANES):
            cols = slice(c, c + LANES)
            entry = nbr_ref[face : face + 1, cols]
            there = entry >= elements
            weight = rows8(jnp.where(there, fscale_ref[face : face + 1, cols], 0.0))
            index = rows8(jnp.where(there, entry - elements, 0))
            for row in range(0, rows, SUB):
                at = rows * face + row
                g_ref[at : at + SUB, cols] = weight * pick(halves[row // SUB], index)


def first_local_kernel(
    counts_ref,
    start_ref,
    right_ref,
    scale_ref,
    fscale_ref,
    nbr_ref,
    elem_ref,
    smooth_ref,
    faces_ref,
    prolong_ref,
    csmooth_ref,
    part_ref,
    folded_ref,
    lead_ref,
    relax_ref,
    source_ref,
    g_ref,
):
    rows, elements = start_ref.shape
    active = activity(counts_ref, elements)
    source_ref[...] = jnp.where(active, right_ref[...], 0.0)
    relax_ref[...] = jnp.where(active, OMEGA / scale_ref[...], 0.0)
    cdof = csmooth_ref.shape[0]
    lead_ref[rows:, :] = smooth_ref[...]
    for at in range(0, prolong_ref.shape[0], cdof):
        lead_ref[at : at + cdof, :] = dot(csmooth_ref[...], prolong_ref[at : at + cdof, :])
    lead = lead_ref[...]
    folded_ref[:, 0:rows] = dot(lead, elem_ref[...])
    for face in range(FACES):
        folded_ref[:, rows * (face + 1) : rows * (face + 2)] = dot(lead, faces_ref[face])
    local_blocks(start_ref, scale_ref, fscale_ref, nbr_ref, g_ref)
    change = dot(smooth_ref[...], source_ref[...]) - dot(folded_ref[rows:, :], g_ref[...])
    part_ref[...] = start_ref[...] + relax_ref[...] * change


def smoothed_kernel(
    part_ref, relax_ref, folded_ref, fscale_ref, nbr_ref, send_ref, p0, p1, p2, p3, smoothed_ref, *rest
):
    outs, g_ref = rest[:4], rest[4]
    rows, elements = part_ref.shape
    ghost_blocks((p0, p1, p2, p3), rows, elements, fscale_ref, nbr_ref, g_ref)
    smoothed_ref[...] = part_ref[...] - relax_ref[...] * dot(folded_ref[rows:, rows:], g_ref[...], HIGHEST)
    pack(send_ref[...], smoothed_ref, outs, rows, elements)
    packets = (p0, p1, p2, p3)
    for slot, axis in enumerate(("wide", "wide", "narrow", "narrow")):
        straight = slot if lax.axis_size(axis) % 2 else slot ^ 1
        relayed = (straight, 2, 3) if axis == "wide" else (straight,)
        for place, which in enumerate(relayed):
            at = rows + SUB * place
            outs[slot][at : at + SUB, :] = packets[which][rows : rows + SUB, :]


def second_local_kernel(
    counts_ref,
    smoothed_ref,
    source_ref,
    scale_ref,
    fscale_ref,
    nbr_ref,
    lead_ref,
    folded_ref,
    prolong_ref,
    slot_ref,
    cscale_ref,
    cfscale_ref,
    cnbr_ref,
    csend_ref,
    p0,
    p1,
    p2,
    p3,
    value_ref,
    spread_ref,
    prol_ref,
    place_ref,
    child_ref,
    weight_ref,
    table_ref,
    g_ref,
    *,
    kids,
):
    rows, elements = smoothed_ref.shape
    coarse = cscale_ref.shape[1]
    local_blocks(smoothed_ref, scale_ref, fscale_ref, nbr_ref, g_ref)
    value_ref[...] = dot(lead_ref[...], source_ref[...]) - dot(folded_ref[...], g_ref[...])

    prol_ref[...] = prolong_ref[...].T
    prol = prol_ref[...]
    for block in range(FACES + 1):
        cols = slice(rows * block, rows * (block + 1))
        spread_ref[:, cols] = dot(folded_ref[rows:, cols], prol)

    active = activity(counts_ref, elements)
    own = jnp.where(active, slot_ref[...], -1)
    halves = received((p0, p1, p2, p3), rows)
    tiles = [rows8(own[:, c : c + LANES].astype(jnp.float32)) for c in range(0, elements, LANES)]
    tiles += [rows8(half[0:1]) for half in halves]
    line = lax.broadcasted_iota(jnp.int32, (SUB, LANES), 0)
    blank = jnp.zeros((SUB - FACES, LANES), jnp.int32)
    side = halves[0].shape[1] // 2
    for c in range(0, elements, LANES):
        cols = slice(c, c + LANES)
        entry = jnp.concatenate([nbr_ref[:, cols], blank], axis=0)
        slot = pick(tiles, jnp.maximum(entry, 0)).astype(jnp.int32)
        slot = jnp.where(line == FACES, rows8(own[:, cols]), slot)
        live = (slot >= 0) & (entry >= 0)
        slot = jnp.where(live, slot, 0)
        group = jnp.where(entry >= elements, 1 + (entry - elements) // side, 0)
        place_ref[:, cols] = group * coarse + slot // kids
        child_ref[:, cols] = slot % kids
        weight = jnp.concatenate([fscale_ref[:, cols], scale_ref[:, cols], scale_ref[:, cols]], axis=0)
        weight_ref[:, cols] = jnp.where(live, weight, 0.0)

    cweight = jnp.where(cnbr_ref[...] >= 0, cfscale_ref[...] * (COARSE_OMEGA / cscale_ref[...]), 0.0)
    sends = jnp.concatenate([csend_ref[i : i + 1].astype(jnp.float32) for i in range(csend_ref.shape[0])], axis=1)
    spare = coarse - sends.shape[1]
    if spare:
        sends = jnp.concatenate([sends, jnp.zeros((1, spare), jnp.float32)], axis=1)
    table_ref[...] = jnp.concatenate([cweight, sends, sends], axis=0)


def restrict_kernel(
    value_ref,
    smoothed_ref,
    relax_ref,
    folded_ref,
    fscale_ref,
    nbr_ref,
    slot_ref,
    cscale_ref,
    table_ref,
    p0,
    p1,
    p2,
    p3,
    base_ref,
    message_ref,
    g_ref,
    *,
    kids,
):
    rows, elements = smoothed_ref.shape
    coarse = cscale_ref.shape[1]
    ghost_blocks((p0, p1, p2, p3), rows, elements, fscale_ref, nbr_ref, g_ref)
    value = value_ref[...] - dot(folded_ref[:, rows:], g_ref[...])
    base_ref[...] = smoothed_ref[...] + relax_ref[...] * value[rows:, :]
    slot = slot_ref[...]
    child = rows8(slot % kids)
    step = rows // kids
    summed = jnp.where(child == 0, value[0:step, :], 0.0)
    for kid in range(1, kids):
        summed = jnp.where(child == kid, value[kid * step : (kid + 1) * step, :], summed)
    member = lax.broadcasted_iota(jnp.int32, (coarse, elements), 0) == slot // kids
    first = dot_t(summed, member.astype(jnp.float32)) * (COARSE_OMEGA / cscale_ref[...])
    message = jnp.concatenate([first, table_ref[...]], axis=1)
    for device in range(message_ref.shape[0]):
        message_ref[device] = message


def neighbourhood(mesh_shape, reach):
    wides, narrows = mesh_shape
    seen, found = set(), []
    near = [(0, 0), (-1, 0), (1, 0), (0, -1), (0, 1)]
    found.extend(near)
    seen.update((w % wides, n % narrows) for w, n in near)
    counts = [1, len(found)]
    for distance in range(2, reach + 1):
        for w in range(-distance, distance + 1):
            for n in (distance - abs(w), abs(w) - distance):
                key = (w % wides, n % narrows)
                if key not in seen:
                    seen.add(key)
                    found.append((w, n))
        counts.append(len(found))
    return found, counts


def neighbour_tables(row, own_ref, near, far):
    def brought(packets, axis, at):
        base = 0 if axis == "wide" else 2
        return in_order(axis, *(packet[at : at + SUB, :] for packet in packets[base : base + 2]))

    own = own_ref[...].astype(jnp.float32)
    found = {(0, 0): jnp.concatenate([jnp.zeros((SUB - FACES, own.shape[1]), jnp.float32), own], axis=0)}
    found[-1, 0], found[1, 0] = brought(near, "wide", row)
    found[0, -1], found[0, 1] = brought(near, "narrow", row)
    found[-2, 0], found[2, 0] = brought(far, "wide", row)
    found[0, -2], found[0, 2] = brought(far, "narrow", row)
    one, two = brought(far, "wide", row + SUB), brought(far, "wide", row + 2 * SUB)
    for side in range(2):
        found[2 * side - 1, -1], found[2 * side - 1, 1] = in_order("narrow", one[side], two[side])
    return found


def paired(pieces):
    if len(pieces) % 2:
        pieces = pieces + [pieces[0]]
    return [jnp.concatenate(pieces[i : i + 2], axis=1) for i in range(0, len(pieces), 2)]


def finish_kernel(
    message_ref,
    base_ref,
    relax_ref,
    prol_ref,
    spread_ref,
    place_ref,
    child_ref,
    weight_ref,
    cblock_ref,
    csmooth_ref,
    cfaces_ref,
    cnbr_ref,
    p0,
    p1,
    p2,
    p3,
    q0,
    q1,
    q2,
    q3,
    field_ref,
    correction_ref,
    folded_ref,
    cg_ref,
    g_ref,
    *,
    mesh_shape,
    kids,
    sent,
):
    rows, elements = base_ref.shape
    cdof, coarse = correction_ref.shape
    wides, narrows = mesh_shape
    offsets, counts = neighbourhood(mesh_shape, 3)
    parts = []
    for w, n in offsets:
        at_w = lax.rem(lax.axis_index("wide") + (w % wides), wides)
        at_n = lax.rem(lax.axis_index("narrow") + (n % narrows), narrows)
        parts.append(at_w * narrows + at_n)
    csmooth = csmooth_ref[...]
    own = COARSE_OMEGA * dot(csmooth, cblock_ref[...])
    for face in range(FACES):
        folded_ref[:, face * cdof : (face + 1) * cdof] = dot(csmooth, cfaces_ref[face])
    folded = folded_ref[...]

    tables = neighbour_tables(rows, cnbr_ref, (p0, p1, p2, p3), (q0, q1, q2, q3))
    ranks = {}
    for rank, (w, n) in reversed(list(enumerate(offsets))):
        ranks[w % wides, n % narrows] = rank
    beside = [
        [ranks[(w + dw) % wides, (n + dn) % narrows] * coarse for dw, dn in offsets[1:5]] for w, n in offsets[: counts[2]]
    ]
    messages = [message_ref[part] for part in parts]
    first = paired([message[:, :coarse] for message in messages])
    extras = paired([message[:, coarse:] for message in messages])
    lists = [rows8(extra[FACES : FACES + 1]) for extra in extras]
    entries = paired([tables[offset] for offset in offsets[: counts[2]]])
    left = lax.broadcasted_iota(jnp.int32, (SUB, LANES), 1) < coarse
    indices = []
    for t, entry in enumerate(entries):
        pair = [2 * t, min(2 * t + 1, counts[2] - 1)]
        entry = jnp.maximum(entry.astype(jnp.int32), 0)
        remote = entry - coarse
        base = [jnp.where(left, beside[pair[0]][d], beside[pair[1]][d]) for d in range(4)]
        owner = jnp.where(
            remote < 2 * sent,
            jnp.where(remote < sent, base[0], base[1]),
            jnp.where(remote < 3 * sent, base[2], base[3]),
        )
        home = jnp.where(left, pair[0] * coarse, pair[1] * coarse)
        there = pick(lists, owner + jnp.maximum(remote, 0)).astype(jnp.int32)
        indices.append(jnp.where(remote < 0, home + entry, owner + there))

    current = first
    for count in (counts[2], counts[1]):
        following = []
        tiles = -(-count // 2)
        for t in range(tiles):
            for face in range(FACES):
                row = SUB - FACES + face
                chosen = pick(current, rows8(indices[t][row : row + 1]))
                cg_ref[face * cdof : (face + 1) * cdof, t * LANES : (t + 1) * LANES] = (
                    rows8(extras[t][face : face + 1]) * chosen
                )
        pulled = dot(folded, cg_ref[:, : tiles * LANES])
        inner = dot(own, jnp.concatenate(current[:tiles], axis=1))
        for t in range(tiles):
            cols = slice(t * LANES, (t + 1) * LANES)
            following.append(current[t] + first[t] - inner[:, cols] - pulled[:, cols])
        current = following
    correction_ref[...] = current[0][:, :coarse]

    for c in range(0, elements, LANES):
        cols = slice(c, c + LANES)
        for row in range(FACES + 1):
            block = 0 if row == FACES else row + 1
            chosen = pick(current, rows8(place_ref[row : row + 1, cols]))
            child = rows8(child_ref[row : row + 1, cols])
            if row == FACES:
                live = rows8(jnp.where(weight_ref[row : row + 1, cols] > 0.0, 1.0, 0.0)) * chosen
                for kid in range(kids):
                    at = (FACES + 1) * rows + kid * cdof
                    g_ref[at : at + cdof, cols] = jnp.where(child == kid, live, 0.0)
            chosen = rows8(weight_ref[row : row + 1, cols]) * chosen
            for kid in range(kids):
                at = block * rows + kid * cdof
                g_ref[at : at + cdof, cols] = jnp.where(child == kid, chosen, 0.0)
    split = (FACES + 1) * rows
    change = dot(spread_ref[...], g_ref[0:split, :])
    delta = dot(prol_ref[...], g_ref[split:, :])
    field_ref[...] = base_ref[...] + delta - relax_ref[...] * change


def swap_routes(size):
    if size % 2:
        return [[(i, (i + 1) % size) for i in range(size)], [(i, (i - 1) % size) for i in range(size)]]
    return [
        [(i, i + 1 if i % 2 == 0 else i - 1) for i in range(size)],
        [(i, (i - 1 if i % 2 == 0 else i + 1) % size) for i in range(size)],
    ]


def exchange(packets):
    moved = []
    for base, axis in ((0, "wide"), (2, "narrow")):
        for half, route in enumerate(swap_routes(lax.axis_size(axis))):
            moved.append(lax.ppermute(packets[base + half], axis, route))
    return moved


SMEM = pl.BlockSpec(memory_space=pltpu.SMEM)
VMEM = pl.BlockSpec(memory_space=pltpu.VMEM)
HBM = pl.BlockSpec(memory_space=pltpu.HBM)


def call(kernel, scalars, arrays, shapes, scratch=(), flops=0, space=VMEM):
    outs = [jax.ShapeDtypeStruct(shape, dtype) for shape, dtype in shapes]
    if space is HBM:
        arrays = [pltpu.with_memory_space_constraint(x, pltpu.HBM) for x in arrays]
    moved = sum(x.size * 4 for x in arrays)
    return pl.pallas_call(
        kernel,
        out_shape=outs,
        in_specs=[SMEM] * len(scalars) + [space] * len(arrays),
        out_specs=[VMEM] * len(outs),
        scratch_shapes=[pltpu.VMEM(x, jnp.float32) if isinstance(x, tuple) else x for x in scratch],
        compiler_params=pltpu.CompilerParams(vmem_limit_bytes=GRANT),
        cost_estimate=pl.CostEstimate(flops=flops, bytes_accessed=moved, transcendentals=0),
    )(*scalars, *arrays)


def body(
    start_field,
    right_side,
    element_scale,
    face_scale,
    face_nbr,
    send_list,
    counts,
    coarse_slot,
    elem_block,
    smooth_block,
    face_blocks,
    prolong,
    coarse_scale,
    coarse_face_scale,
    coarse_nbr,
    coarse_send,
    coarse_block,
    coarse_smooth,
    coarse_faces,
):
    rows, elements = start_field.shape
    kids, _, cdof = prolong.shape
    prolong = prolong.transpose(0, 2, 1).reshape(kids * cdof, rows)
    coarse = coarse_scale.shape[0]
    sent = send_list.shape[1]
    mesh_shape = (lax.axis_size("wide"), lax.axis_size("narrow"))
    devices = mesh_shape[0] * mesh_shape[1]
    f32, i32 = jnp.float32, jnp.int32
    scale = element_scale.reshape(1, elements)
    slot = coarse_slot.reshape(1, elements)
    cscale = coarse_scale.reshape(1, coarse)
    blocks = (FACES + 1) * rows

    kept = (
        slot,
        coarse_nbr,
        coarse_send,
        right_side,
        scale,
        face_scale,
        face_nbr,
        elem_block,
        smooth_block,
        face_blocks,
        prolong,
        cscale,
        coarse_face_scale,
        coarse_block,
        coarse_smooth,
        coarse_faces,
        send_list,
    )
    start, *brought = call(
        functools.partial(start_kernel, carried=len(kept)),
        (counts,),
        (start_field, send_list, *kept),
        [((rows, elements), f32)] + [((rows + SUB, sent), f32)] * 4 + [(x.shape, x.dtype) for x in kept],
        [
            pltpu.VMEM(start_field.shape, f32),
            pltpu.VMEM(send_list.shape, i32),
            pltpu.SemaphoreType.DMA((len(kept) + 2,)),
        ],
        space=HBM,
    )
    packets = brought[:4]
    (
        slot,
        coarse_nbr,
        coarse_send,
        right_side,
        scale,
        face_scale,
        face_nbr,
        elem_block,
        smooth_block,
        face_blocks,
        prolong,
        cscale,
        coarse_face_scale,
        coarse_block,
        coarse_smooth,
        coarse_faces,
        send_list,
    ) = brought[4:]
    first_ghosts = exchange(packets)
    part, folded, lead, relax, source = call(
        first_local_kernel,
        (counts,),
        (
            start,
            right_side,
            scale,
            face_scale,
            face_nbr,
            elem_block,
            smooth_block,
            face_blocks,
            prolong,
            coarse_smooth,
        ),
        [
            ((rows, elements), f32),
            ((2 * rows, blocks), f32),
            ((2 * rows, rows), f32),
            ((1, elements), f32),
            ((rows, elements), f32),
        ],
        [(blocks, elements)],
        flops=2 * blocks * rows * elements,
    )
    smoothed, *packets = call(
        smoothed_kernel,
        (),
        (part, relax, folded, face_scale, face_nbr, send_list, *first_ghosts),
        [((rows, elements), f32)] + [((rows + 3 * SUB, sent), f32)] * 2 + [((rows + SUB, sent), f32)] * 2,
        [(blocks - rows, elements)],
        flops=2 * blocks * rows * elements,
    )
    second_ghosts = exchange(packets)
    value, spread, prol, place, child, weight, table = call(
        functools.partial(second_local_kernel, kids=kids),
        (counts,),
        (
            smoothed,
            source,
            scale,
            face_scale,
            face_nbr,
            lead,
            folded,
            prolong,
            slot,
            cscale,
            coarse_face_scale,
            coarse_nbr,
            coarse_send,
            *first_ghosts,
        ),
        [
            ((2 * rows, elements), f32),
            ((rows, blocks), f32),
            ((rows, kids * cdof), f32),
            ((SUB, elements), i32),
            ((SUB, elements), i32),
            ((SUB, elements), f32),
            ((SUB, coarse), f32),
        ],
        [(blocks, elements)],
        flops=4 * blocks * rows * elements,
    )
    base, message = call(
        functools.partial(restrict_kernel, kids=kids),
        (),
        (value, smoothed, relax, folded, face_scale, face_nbr, slot, cscale, table, *second_ghosts),
        [((rows, elements), f32), ((devices, SUB, 2 * coarse), f32)],
        [(blocks - rows, elements)],
        flops=4 * blocks * rows * elements,
    )
    gathered = lax.all_to_all(message, ("wide", "narrow"), 0, 0)
    needed = -(-neighbourhood(mesh_shape, 3)[1][2] // 2) * 2 * coarse
    return tuple(
        call(
            functools.partial(finish_kernel, mesh_shape=mesh_shape, kids=kids, sent=coarse_send.shape[1]),
            (),
            (
                gathered,
                base,
                relax,
                prol,
                spread,
                place,
                child,
                weight,
                coarse_block,
                coarse_smooth,
                coarse_faces,
                coarse_nbr,
                *first_ghosts,
                *second_ghosts,
            ),
            [((rows, elements), f32), ((cdof, coarse), f32)],
            [(cdof, FACES * cdof), (FACES * cdof, needed), (blocks + rows, elements)],
            flops=2 * blocks * rows * elements,
        )
    )


def solution(mesh):
    both = ("wide", "narrow")

    return jax.shard_map(
        body,
        mesh=mesh,
        in_specs=(
            P(None, both),
            P(None, both),
            P(both),
            P(None, both),
            P(None, both),
            P(None, both),
            P(both),
            P(both),
            P(),
            P(),
            P(),
            P(),
            P(both),
            P(None, both),
            P(None, both),
            P(None, both),
            P(),
            P(),
            P(),
        ),
        out_specs=(P(None, both), P(None, both)),
        check_vma=False,
    )
```

```python
import functools

import jax
import jax.numpy as jnp
from jax import lax
from jax.experimental import pallas as pl
from jax.experimental.pallas import tpu as pltpu
from jax.sharding import PartitionSpec as P


OMEGA = 0.7
COARSE_OMEGA = 0.6
HIGH = lax.Precision.HIGH
HIGHEST = lax.Precision.HIGHEST
LANES = 128
SUB = 8
FACES = 6
GRANT = 16 * 1024 * 1024


def dot(left, right, precision=HIGH):
    return jnp.dot(left, right, preferred_element_type=jnp.float32, precision=precision)


def dot_t(left, right):
    return lax.dot_general(
        left, right, (((1,), (1,)), ((), ())), preferred_element_type=jnp.float32, precision=HIGH
    )


def lane_take(tile, index):
    return jnp.take_along_axis(tile, index, axis=1, mode="promise_in_bounds")


def pick(tiles, index):
    low = index & (LANES - 1)
    high = index >> 7
    found = lane_take(tiles[0], low)
    for place in range(1, len(tiles)):
        found = jnp.where(high == place, lane_take(tiles[place], low), found)
    return found


def rows8(row):
    return jnp.broadcast_to(row, (SUB, row.shape[1]))


def swapped(axis, one, other):
    if lax.axis_size(axis) % 2:
        return one, other
    odd = lax.rem(lax.axis_index(axis), 2) != 0
    return jnp.where(odd, other, one), jnp.where(odd, one, other)


def activity(counts_ref, elements):
    lane = lax.broadcasted_iota(jnp.int32, (1, elements), 1)
    return lane < counts_ref[0]


def ordered_sends(send):
    out = []
    for base, axis in ((0, "wide"), (2, "narrow")):
        out.extend(swapped(axis, send[base : base + 1], send[base + 1 : base + 2]))
    return out


def store_packets(outs, halves, row):
    size = outs[0].shape[1]
    for half, tile in enumerate(halves):
        outs[2 * half][row : row + SUB, :] = tile[:, :size]
        outs[2 * half + 1][row : row + SUB, :] = tile[:, size : 2 * size]


def pack(send, source_ref, outs, rows, elements):
    order = ordered_sends(send)
    index = [rows8(jnp.concatenate(order[:2], axis=1)), rows8(jnp.concatenate(order[2:], axis=1))]
    for row in range(0, rows, SUB):
        tiles = [source_ref[row : row + SUB, c : c + LANES] for c in range(0, elements, LANES)]
        store_packets(outs, [pick(tiles, which) for which in index], row)
    return index


def in_order(axis, first, second):
    if lax.axis_size(axis) % 2:
        return first, second
    return swapped(axis, second, first)


def received(packets, row):
    tiles = []
    for base, axis in ((0, "wide"), (2, "narrow")):
        pair = [packet[row : row + SUB, :] for packet in packets[base : base + 2]]
        tiles.append(jnp.concatenate(in_order(axis, *pair), axis=1))
    return tiles


def start_kernel(counts_ref, *refs, carried):
    given, refs = refs[: carried + 2], refs[carried + 2 :]
    masked_ref, outs, kept = refs[0], refs[1:5], refs[5 : 5 + carried]
    start_ref, send_ref, sems = refs[5 + carried :]
    slot_ref, cnbr_ref, csend_ref = kept[:3]
    held = (start_ref, send_ref, *kept)
    copies = [pltpu.make_async_copy(here, there, sems.at[i]) for i, (here, there) in enumerate(zip(given, held))]
    for copy in copies:
        copy.start()
    for copy in copies[:5]:
        copy.wait()
    rows, elements = start_ref.shape
    active = activity(counts_ref, elements)
    masked_ref[...] = jnp.where(active, start_ref[...], 0.0)
    index = pack(send_ref[...], masked_ref, outs, rows, elements)
    slots = rows8(jnp.where(active, slot_ref[...], -1).astype(jnp.float32))
    tiles = [slots[:, c : c + LANES] for c in range(0, elements, LANES)]
    csend = csend_ref[...].astype(jnp.float32)
    blank = jnp.zeros((1, LANES // 2 - csend.shape[1]), jnp.float32)
    order = ordered_sends(csend)
    table = cnbr_ref[...].astype(jnp.float32)
    table = jnp.concatenate([table, table], axis=1)
    halves = []
    for half in range(2):
        coarse = jnp.concatenate([order[2 * half], blank, order[2 * half + 1], blank], axis=1)
        halves.append(jnp.concatenate([pick(tiles, index[half])[0:1], coarse, table], axis=0))
    store_packets(outs, halves, rows)
    for copy in copies[5:]:
        copy.wait()


def local_blocks(current_ref, scale_ref, fscale_ref, nbr_ref, g_ref):
    rows, elements = current_ref.shape
    for c in range(0, elements, LANES):
        cols = slice(c, c + LANES)
        g_ref[0:rows, cols] = current_ref[:, cols] * scale_ref[:, cols]
    for face in range(FACES):
        for c in range(0, elements, LANES):
            cols = slice(c, c + LANES)
            entry = nbr_ref[face : face + 1, cols]
            here = (entry >= 0) & (entry < elements)
            weight = rows8(jnp.where(here, fscale_ref[face : face + 1, cols], 0.0))
            index = rows8(jnp.where(here, entry, 0))
            for row in range(0, rows, SUB):
                tiles = [current_ref[row : row + SUB, k : k + LANES] for k in range(0, elements, LANES)]
                at = rows * (face + 1) + row
                g_ref[at : at + SUB, cols] = weight * pick(tiles, index)


def ghost_tables(fscale_ref, nbr_ref, index_ref, early_ref, late_ref, sent):
    entry = nbr_ref[...] - fscale_ref.shape[1]
    way = jnp.maximum(entry, 0) // sent
    narrow = way // 2
    index_ref[...] = jnp.where(entry >= 0, narrow * sent + way * (-sent) + entry, 0)
    flips = []
    for axis in ("wide", "narrow"):
        even = lax.axis_size(axis) % 2 == 0
        flips.append(1 - lax.rem(lax.axis_index(axis), 2) if even else jnp.int32(0))
    swap = (way & 1) ^ jnp.where(narrow == 0, flips[0], flips[1])
    weight = jnp.where(entry >= 0, fscale_ref[...], 0.0)
    early_ref[...] = jnp.where(swap == 0, weight, 0.0)
    late_ref[...] = jnp.where(swap == 0, 0.0, weight)


def ghost_blocks(wide_ref, narrow_ref, rows, index_ref, weight_ref, g_ref, before_ref=None):
    halves = [
        jnp.concatenate([wide_ref[row : row + SUB, :], narrow_ref[row : row + SUB, :]], axis=1)
        for row in range(0, rows, SUB)
    ]
    for face in range(FACES):
        for c in range(0, index_ref.shape[1], LANES):
            cols = slice(c, c + LANES)
            weight = rows8(weight_ref[face : face + 1, cols])
            index = rows8(index_ref[face : face + 1, cols])
            for row in range(0, rows, SUB):
                at = rows * face + row
                value = weight * lane_take(halves[row // SUB], index)
                if before_ref is not None:
                    value = value + before_ref[at : at + SUB, cols]
                g_ref[at : at + SUB, cols] = value


def early_kernel(index_ref, weight_ref, wide_ref, narrow_ref, g_ref):
    ghost_blocks(wide_ref, narrow_ref, g_ref.shape[0] // FACES, index_ref, weight_ref, g_ref)


def first_local_kernel(
    counts_ref,
    start_ref,
    right_ref,
    scale_ref,
    fscale_ref,
    nbr_ref,
    elem_ref,
    smooth_ref,
    faces_ref,
    prolong_ref,
    csmooth_ref,
    part_ref,
    folded_ref,
    lead_ref,
    relax_ref,
    source_ref,
    index_ref,
    early_ref,
    late_ref,
    g_ref,
    *,
    sent,
):
    rows, elements = start_ref.shape
    ghost_tables(fscale_ref, nbr_ref, index_ref, early_ref, late_ref, sent)
    active = activity(counts_ref, elements)
    source_ref[...] = jnp.where(active, right_ref[...], 0.0)
    relax_ref[...] = jnp.where(active, OMEGA / scale_ref[...], 0.0)
    cdof = csmooth_ref.shape[0]
    lead_ref[rows:, :] = smooth_ref[...]
    for at in range(0, prolong_ref.shape[0], cdof):
        lead_ref[at : at + cdof, :] = dot(csmooth_ref[...], prolong_ref[at : at + cdof, :], HIGHEST)
    lead = lead_ref[...]
    folded_ref[:, 0:rows] = dot(lead, elem_ref[...], HIGHEST)
    for face in range(FACES):
        folded_ref[:, rows * (face + 1) : rows * (face + 2)] = dot(lead, faces_ref[face], HIGHEST)
    local_blocks(start_ref, scale_ref, fscale_ref, nbr_ref, g_ref)
    change = dot(smooth_ref[...], source_ref[...], HIGHEST) - dot(folded_ref[rows:, :], g_ref[...], HIGHEST)
    part_ref[...] = start_ref[...] + relax_ref[...] * change


def smoothed_kernel(
    part_ref, relax_ref, folded_ref, index_ref, late_ref, early_ref, send_ref, p0, p1, p2, p3, smoothed_ref, *rest
):
    outs, g_ref = rest[:4], rest[4]
    rows, elements = part_ref.shape
    ghost_blocks(p1, p3, rows, index_ref, late_ref, g_ref, early_ref)
    smoothed_ref[...] = part_ref[...] - relax_ref[...] * dot(folded_ref[rows:, rows:], g_ref[...], HIGHEST)
    pack(send_ref[...], smoothed_ref, outs, rows, elements)
    packets = (p0, p1, p2, p3)
    for slot, axis in enumerate(("wide", "wide", "narrow", "narrow")):
        straight = slot if lax.axis_size(axis) % 2 else slot ^ 1
        relayed = (straight, 2, 3) if axis == "wide" else (straight,)
        for place, which in enumerate(relayed):
            at = rows + SUB * place
            outs[slot][at : at + SUB, :] = packets[which][rows : rows + SUB, :]


def second_local_kernel(
    counts_ref,
    smoothed_ref,
    source_ref,
    scale_ref,
    fscale_ref,
    nbr_ref,
    lead_ref,
    folded_ref,
    prolong_ref,
    slot_ref,
    cscale_ref,
    cfscale_ref,
    cnbr_ref,
    csend_ref,
    p0,
    p1,
    p2,
    p3,
    value_ref,
    spread_ref,
    prol_ref,
    place_ref,
    child_ref,
    weight_ref,
    table_ref,
    g_ref,
    *,
    kids,
):
    rows, elements = smoothed_ref.shape
    coarse = cscale_ref.shape[1]
    local_blocks(smoothed_ref, scale_ref, fscale_ref, nbr_ref, g_ref)
    value_ref[...] = dot(lead_ref[...], source_ref[...], HIGHEST) - dot(folded_ref[...], g_ref[...], HIGHEST)

    prol_ref[...] = prolong_ref[...].T
    prol = prol_ref[...]
    for block in range(FACES + 1):
        cols = slice(rows * block, rows * (block + 1))
        spread_ref[:, cols] = dot(folded_ref[rows:, cols], prol, HIGHEST)

    active = activity(counts_ref, elements)
    own = jnp.where(active, slot_ref[...], -1)
    halves = received((p0, p1, p2, p3), rows)
    tiles = [rows8(own[:, c : c + LANES].astype(jnp.float32)) for c in range(0, elements, LANES)]
    tiles += [rows8(half[0:1]) for half in halves]
    line = lax.broadcasted_iota(jnp.int32, (SUB, LANES), 0)
    blank = jnp.zeros((SUB - FACES, LANES), jnp.int32)
    side = halves[0].shape[1] // 2
    for c in range(0, elements, LANES):
        cols = slice(c, c + LANES)
        entry = jnp.concatenate([nbr_ref[:, cols], blank], axis=0)
        slot = pick(tiles, jnp.maximum(entry, 0)).astype(jnp.int32)
        slot = jnp.where(line == FACES, rows8(own[:, cols]), slot)
        live = (slot >= 0) & (entry >= 0)
        slot = jnp.where(live, slot, 0)
        group = jnp.where(entry >= elements, 1 + (entry - elements) // side, 0)
        place_ref[:, cols] = group * coarse + slot // kids
        child_ref[:, cols] = slot % kids
        weight = jnp.concatenate([fscale_ref[:, cols], scale_ref[:, cols], scale_ref[:, cols]], axis=0)
        weight_ref[:, cols] = jnp.where(live, weight, 0.0)

    cweight = jnp.where(cnbr_ref[...] >= 0, cfscale_ref[...] * (COARSE_OMEGA / cscale_ref[...]), 0.0)
    sends = jnp.concatenate([csend_ref[i : i + 1].astype(jnp.float32) for i in range(csend_ref.shape[0])], axis=1)
    spare = coarse - sends.shape[1]
    if spare:
        sends = jnp.concatenate([sends, jnp.zeros((1, spare), jnp.float32)], axis=1)
    table_ref[...] = jnp.concatenate([cweight, sends, sends], axis=0)


def restrict_kernel(
    value_ref,
    smoothed_ref,
    relax_ref,
    folded_ref,
    index_ref,
    late_ref,
    early_ref,
    slot_ref,
    cscale_ref,
    table_ref,
    wide_ref,
    narrow_ref,
    base_ref,
    message_ref,
    g_ref,
    *,
    kids,
):
    rows, elements = smoothed_ref.shape
    coarse = cscale_ref.shape[1]
    ghost_blocks(wide_ref, narrow_ref, rows, index_ref, late_ref, g_ref, early_ref)
    value = value_ref[...] - dot(folded_ref[:, rows:], g_ref[...])
    base_ref[...] = smoothed_ref[...] + relax_ref[...] * value[rows:, :]
    slot = slot_ref[...]
    child = rows8(slot % kids)
    step = rows // kids
    summed = jnp.where(child == 0, value[0:step, :], 0.0)
    for kid in range(1, kids):
        summed = jnp.where(child == kid, value[kid * step : (kid + 1) * step, :], summed)
    member = lax.broadcasted_iota(jnp.int32, (coarse, elements), 0) == slot // kids
    first = dot_t(summed, member.astype(jnp.float32)) * (COARSE_OMEGA / cscale_ref[...])
    message = jnp.concatenate([first, table_ref[...]], axis=1)
    for device in range(message_ref.shape[0]):
        message_ref[device] = message


def neighbourhood(mesh_shape, reach):
    wides, narrows = mesh_shape
    seen, found = set(), []
    near = [(0, 0), (-1, 0), (1, 0), (0, -1), (0, 1)]
    found.extend(near)
    seen.update((w % wides, n % narrows) for w, n in near)
    counts = [1, len(found)]
    for distance in range(2, reach + 1):
        for w in range(-distance, distance + 1):
            for n in (distance - abs(w), abs(w) - distance):
                key = (w % wides, n % narrows)
                if key not in seen:
                    seen.add(key)
                    found.append((w, n))
        counts.append(len(found))
    return found, counts


def neighbour_tables(row, own_ref, near, far):
    def brought(packets, axis, at):
        base = 0 if axis == "wide" else 2
        return in_order(axis, *(packet[at : at + SUB, :] for packet in packets[base : base + 2]))

    own = own_ref[...].astype(jnp.float32)
    found = {(0, 0): jnp.concatenate([jnp.zeros((SUB - FACES, own.shape[1]), jnp.float32), own], axis=0)}
    found[-1, 0], found[1, 0] = brought(near, "wide", row)
    found[0, -1], found[0, 1] = brought(near, "narrow", row)
    found[-2, 0], found[2, 0] = brought(far, "wide", row)
    found[0, -2], found[0, 2] = brought(far, "narrow", row)
    one, two = brought(far, "wide", row + SUB), brought(far, "wide", row + 2 * SUB)
    for side in range(2):
        found[2 * side - 1, -1], found[2 * side - 1, 1] = in_order("narrow", one[side], two[side])
    return found


def paired(pieces):
    if len(pieces) % 2:
        pieces = pieces + [pieces[0]]
    return [jnp.concatenate(pieces[i : i + 2], axis=1) for i in range(0, len(pieces), 2)]


def finish_kernel(
    message_ref,
    base_ref,
    relax_ref,
    prol_ref,
    spread_ref,
    place_ref,
    child_ref,
    weight_ref,
    cblock_ref,
    csmooth_ref,
    cfaces_ref,
    cnbr_ref,
    p0,
    p1,
    p2,
    p3,
    q0,
    q1,
    q2,
    q3,
    field_ref,
    correction_ref,
    folded_ref,
    cg_ref,
    g_ref,
    *,
    mesh_shape,
    kids,
    sent,
):
    rows, elements = base_ref.shape
    cdof, coarse = correction_ref.shape
    wides, narrows = mesh_shape
    offsets, counts = neighbourhood(mesh_shape, 3)
    parts = []
    for w, n in offsets:
        at_w = lax.rem(lax.axis_index("wide") + (w % wides), wides)
        at_n = lax.rem(lax.axis_index("narrow") + (n % narrows), narrows)
        parts.append(at_w * narrows + at_n)
    csmooth = csmooth_ref[...]
    own = COARSE_OMEGA * dot(csmooth, cblock_ref[...])
    for face in range(FACES):
        folded_ref[:, face * cdof : (face + 1) * cdof] = dot(csmooth, cfaces_ref[face])
    folded = folded_ref[...]

    tables = neighbour_tables(rows, cnbr_ref, (p0, p1, p2, p3), (q0, q1, q2, q3))
    ranks = {}
    for rank, (w, n) in reversed(list(enumerate(offsets))):
        ranks[w % wides, n % narrows] = rank
    beside = [
        [ranks[(w + dw) % wides, (n + dn) % narrows] * coarse for dw, dn in offsets[1:5]] for w, n in offsets[: counts[2]]
    ]
    messages = [message_ref[part] for part in parts]
    first = paired([message[:, :coarse] for message in messages])
    extras = paired([message[:, coarse:] for message in messages])
    lists = [rows8(extra[FACES : FACES + 1]) for extra in extras]
    entries = paired([tables[offset] for offset in offsets[: counts[2]]])
    left = lax.broadcasted_iota(jnp.int32, (SUB, LANES), 1) < coarse
    indices = []
    for t, entry in enumerate(entries):
        pair = [2 * t, min(2 * t + 1, counts[2] - 1)]
        entry = jnp.maximum(entry.astype(jnp.int32), 0)
        remote = entry - coarse
        base = [jnp.where(left, beside[pair[0]][d], beside[pair[1]][d]) for d in range(4)]
        owner = jnp.where(
            remote < 2 * sent,
            jnp.where(remote < sent, base[0], base[1]),
            jnp.where(remote < 3 * sent, base[2], base[3]),
        )
        home = jnp.where(left, pair[0] * coarse, pair[1] * coarse)
        there = pick(lists, owner + jnp.maximum(remote, 0)).astype(jnp.int32)
        indices.append(jnp.where(remote < 0, home + entry, owner + there))

    current = first
    for count in (counts[2], counts[1]):
        following = []
        tiles = -(-count // 2)
        for t in range(tiles):
            for face in range(FACES):
                row = SUB - FACES + face
                chosen = pick(current, rows8(indices[t][row : row + 1]))
                cg_ref[face * cdof : (face + 1) * cdof, t * LANES : (t + 1) * LANES] = (
                    rows8(extras[t][face : face + 1]) * chosen
                )
        pulled = dot(folded, cg_ref[:, : tiles * LANES])
        inner = dot(own, jnp.concatenate(current[:tiles], axis=1))
        for t in range(tiles):
            cols = slice(t * LANES, (t + 1) * LANES)
            following.append(current[t] + first[t] - inner[:, cols] - pulled[:, cols])
        current = following
    correction_ref[...] = current[0][:, :coarse]

    for c in range(0, elements, LANES):
        cols = slice(c, c + LANES)
        for row in range(FACES + 1):
            block = 0 if row == FACES else row + 1
            chosen = pick(current, rows8(place_ref[row : row + 1, cols]))
            child = rows8(child_ref[row : row + 1, cols])
            if row == FACES:
                live = rows8(jnp.where(weight_ref[row : row + 1, cols] > 0.0, 1.0, 0.0)) * chosen
                for kid in range(kids):
                    at = (FACES + 1) * rows + kid * cdof
                    g_ref[at : at + cdof, cols] = jnp.where(child == kid, live, 0.0)
            chosen = rows8(weight_ref[row : row + 1, cols]) * chosen
            for kid in range(kids):
                at = block * rows + kid * cdof
                g_ref[at : at + cdof, cols] = jnp.where(child == kid, chosen, 0.0)
    split = (FACES + 1) * rows
    change = dot(spread_ref[...], g_ref[0:split, :])
    delta = dot(prol_ref[...], g_ref[split:, :])
    field_ref[...] = base_ref[...] + delta - relax_ref[...] * change


def swap_routes(size):
    if size % 2:
        return [[(i, (i + 1) % size) for i in range(size)], [(i, (i - 1) % size) for i in range(size)]]
    return [
        [(i, i + 1 if i % 2 == 0 else i - 1) for i in range(size)],
        [(i, (i - 1 if i % 2 == 0 else i + 1) % size) for i in range(size)],
    ]


def exchange(packets):
    moved = []
    for base, axis in ((0, "wide"), (2, "narrow")):
        for half, route in enumerate(swap_routes(lax.axis_size(axis))):
            moved.append(lax.ppermute(packets[base + half], axis, route))
    return moved


SMEM = pl.BlockSpec(memory_space=pltpu.SMEM)
VMEM = pl.BlockSpec(memory_space=pltpu.VMEM)
HBM = pl.BlockSpec(memory_space=pltpu.HBM)


def call(kernel, scalars, arrays, shapes, scratch=(), flops=0, space=VMEM):
    outs = [jax.ShapeDtypeStruct(shape, dtype) for shape, dtype in shapes]
    if space is HBM:
        arrays = [pltpu.with_memory_space_constraint(x, pltpu.HBM) for x in arrays]
    moved = sum(x.size * 4 for x in arrays)
    return pl.pallas_call(
        kernel,
        out_shape=outs,
        in_specs=[SMEM] * len(scalars) + [space] * len(arrays),
        out_specs=[VMEM] * len(outs),
        scratch_shapes=[pltpu.VMEM(x, jnp.float32) if isinstance(x, tuple) else x for x in scratch],
        compiler_params=pltpu.CompilerParams(vmem_limit_bytes=GRANT),
        cost_estimate=pl.CostEstimate(flops=flops, bytes_accessed=moved, transcendentals=0),
    )(*scalars, *arrays)


def body(
    start_field,
    right_side,
    element_scale,
    face_scale,
    face_nbr,
    send_list,
    counts,
    coarse_slot,
    elem_block,
    smooth_block,
    face_blocks,
    prolong,
    coarse_scale,
    coarse_face_scale,
    coarse_nbr,
    coarse_send,
    coarse_block,
    coarse_smooth,
    coarse_faces,
):
    rows, elements = start_field.shape
    kids, _, cdof = prolong.shape
    prolong = prolong.transpose(0, 2, 1).reshape(kids * cdof, rows)
    coarse = coarse_scale.shape[0]
    sent = send_list.shape[1]
    mesh_shape = (lax.axis_size("wide"), lax.axis_size("narrow"))
    devices = mesh_shape[0] * mesh_shape[1]
    f32, i32 = jnp.float32, jnp.int32
    scale = element_scale.reshape(1, elements)
    slot = coarse_slot.reshape(1, elements)
    cscale = coarse_scale.reshape(1, coarse)
    blocks = (FACES + 1) * rows

    kept = (
        slot,
        coarse_nbr,
        coarse_send,
        right_side,
        scale,
        face_scale,
        face_nbr,
        elem_block,
        smooth_block,
        face_blocks,
        prolong,
        cscale,
        coarse_face_scale,
        coarse_block,
        coarse_smooth,
        coarse_faces,
        send_list,
    )
    start, *brought = call(
        functools.partial(start_kernel, carried=len(kept)),
        (counts,),
        (start_field, send_list, *kept),
        [((rows, elements), f32)] + [((rows + SUB, sent), f32)] * 4 + [(x.shape, x.dtype) for x in kept],
        [
            pltpu.VMEM(start_field.shape, f32),
            pltpu.VMEM(send_list.shape, i32),
            pltpu.SemaphoreType.DMA((len(kept) + 2,)),
        ],
        space=HBM,
    )
    packets = brought[:4]
    (
        slot,
        coarse_nbr,
        coarse_send,
        right_side,
        scale,
        face_scale,
        face_nbr,
        elem_block,
        smooth_block,
        face_blocks,
        prolong,
        cscale,
        coarse_face_scale,
        coarse_block,
        coarse_smooth,
        coarse_faces,
        send_list,
    ) = brought[4:]
    first_ghosts = exchange(packets)
    part, folded, lead, relax, source, ghost_index, early_weight, late_weight = call(
        functools.partial(first_local_kernel, sent=sent),
        (counts,),
        (
            start,
            right_side,
            scale,
            face_scale,
            face_nbr,
            elem_block,
            smooth_block,
            face_blocks,
            prolong,
            coarse_smooth,
        ),
        [
            ((rows, elements), f32),
            ((2 * rows, blocks), f32),
            ((2 * rows, rows), f32),
            ((1, elements), f32),
            ((rows, elements), f32),
            ((FACES, elements), i32),
            ((FACES, elements), f32),
            ((FACES, elements), f32),
        ],
        [(blocks, elements)],
        flops=2 * blocks * rows * elements,
    )
    early = call(
        early_kernel,
        (),
        (ghost_index, early_weight, first_ghosts[0], first_ghosts[2]),
        [((blocks - rows, elements), f32)],
        flops=blocks * elements,
    )[0]
    smoothed, *packets = call(
        smoothed_kernel,
        (),
        (part, relax, folded, ghost_index, late_weight, early, send_list, *first_ghosts),
        [((rows, elements), f32)] + [((rows + 3 * SUB, sent), f32)] * 2 + [((rows + SUB, sent), f32)] * 2,
        [(blocks - rows, elements)],
        flops=2 * blocks * rows * elements,
    )
    second_ghosts = exchange(packets)
    value, spread, prol, place, child, weight, table = call(
        functools.partial(second_local_kernel, kids=kids),
        (counts,),
        (
            smoothed,
            source,
            scale,
            face_scale,
            face_nbr,
            lead,
            folded,
            prolong,
            slot,
            cscale,
            coarse_face_scale,
            coarse_nbr,
            coarse_send,
            *first_ghosts,
        ),
        [
            ((2 * rows, elements), f32),
            ((rows, blocks), f32),
            ((rows, kids * cdof), f32),
            ((SUB, elements), i32),
            ((SUB, elements), i32),
            ((SUB, elements), f32),
            ((SUB, coarse), f32),
        ],
        [(blocks, elements)],
        flops=4 * blocks * rows * elements,
    )
    early = call(
        early_kernel,
        (),
        (ghost_index, early_weight, second_ghosts[0], second_ghosts[2]),
        [((blocks - rows, elements), f32)],
        flops=blocks * elements,
    )[0]
    base, message = call(
        functools.partial(restrict_kernel, kids=kids),
        (),
        (value, smoothed, relax, folded, ghost_index, late_weight, early, slot, cscale, table, second_ghosts[1], second_ghosts[3]),
        [((rows, elements), f32), ((devices, SUB, 2 * coarse), f32)],
        [(blocks - rows, elements)],
        flops=4 * blocks * rows * elements,
    )
    gathered = lax.all_to_all(message, ("wide", "narrow"), 0, 0)
    needed = -(-neighbourhood(mesh_shape, 3)[1][2] // 2) * 2 * coarse
    return tuple(
        call(
            functools.partial(finish_kernel, mesh_shape=mesh_shape, kids=kids, sent=coarse_send.shape[1]),
            (),
            (
                gathered,
                base,
                relax,
                prol,
                spread,
                place,
                child,
                weight,
                coarse_block,
                coarse_smooth,
                coarse_faces,
                coarse_nbr,
                *first_ghosts,
                *second_ghosts,
            ),
            [((rows, elements), f32), ((cdof, coarse), f32)],
            [(cdof, FACES * cdof), (FACES * cdof, needed), (blocks + rows, elements)],
            flops=2 * blocks * rows * elements,
        )
    )


def solution(mesh):
    both = ("wide", "narrow")

    return jax.shard_map(
        body,
        mesh=mesh,
        in_specs=(
            P(None, both),
            P(None, both),
            P(both),
            P(None, both),
            P(None, both),
            P(None, both),
            P(both),
            P(both),
            P(),
            P(),
            P(),
            P(),
            P(both),
            P(None, both),
            P(None, both),
            P(None, both),
            P(),
            P(),
            P(),
        ),
        out_specs=(P(None, both), P(None, both)),
        check_vma=False,
    )
```

```python
import functools

import jax
import jax.numpy as jnp
from jax import lax
from jax.experimental import pallas as pl
from jax.experimental.pallas import tpu as pltpu
from jax.sharding import PartitionSpec as P


OMEGA = 0.7
COARSE_OMEGA = 0.6
HIGH = lax.Precision.HIGH
HIGHEST = lax.Precision.HIGHEST
LANES = 128
SUB = 8
FACES = 6
GRANT = 16 * 1024 * 1024


def dot(left, right, precision=HIGH):
    return jnp.dot(left, right, preferred_element_type=jnp.float32, precision=precision)


def dot_t(left, right):
    return lax.dot_general(
        left, right, (((1,), (1,)), ((), ())), preferred_element_type=jnp.float32, precision=HIGH
    )


def lane_take(tile, index):
    return jnp.take_along_axis(tile, index, axis=1, mode="promise_in_bounds")


def pick(tiles, index):
    low = index & (LANES - 1)
    high = index >> 7
    found = lane_take(tiles[0], low)
    for place in range(1, len(tiles)):
        found = jnp.where(high == place, lane_take(tiles[place], low), found)
    return found


def rows8(row):
    return jnp.broadcast_to(row, (SUB, row.shape[1]))


def swapped(axis, one, other):
    if lax.axis_size(axis) % 2:
        return one, other
    odd = lax.rem(lax.axis_index(axis), 2) != 0
    return jnp.where(odd, other, one), jnp.where(odd, one, other)


def activity(counts_ref, elements):
    lane = lax.broadcasted_iota(jnp.int32, (1, elements), 1)
    return lane < counts_ref[0]


def ordered_sends(send):
    out = []
    for base, axis in ((0, "wide"), (2, "narrow")):
        out.extend(swapped(axis, send[base : base + 1], send[base + 1 : base + 2]))
    return out


def store_packets(outs, halves, row):
    size = outs[0].shape[1]
    for half, tile in enumerate(halves):
        outs[2 * half][row : row + SUB, :] = tile[:, :size]
        outs[2 * half + 1][row : row + SUB, :] = tile[:, size : 2 * size]


def pack(send, source_ref, outs, rows, elements):
    order = ordered_sends(send)
    index = [rows8(jnp.concatenate(order[:2], axis=1)), rows8(jnp.concatenate(order[2:], axis=1))]
    for row in range(0, rows, SUB):
        tiles = [source_ref[row : row + SUB, c : c + LANES] for c in range(0, elements, LANES)]
        store_packets(outs, [pick(tiles, which) for which in index], row)
    return index


def in_order(axis, first, second):
    if lax.axis_size(axis) % 2:
        return first, second
    return swapped(axis, second, first)


def received(packets, row):
    tiles = []
    for base, axis in ((0, "wide"), (2, "narrow")):
        pair = [packet[row : row + SUB, :] for packet in packets[base : base + 2]]
        tiles.append(jnp.concatenate(in_order(axis, *pair), axis=1))
    return tiles


def start_kernel(counts_ref, *refs, carried):
    given, refs = refs[: carried + 2], refs[carried + 2 :]
    masked_ref, outs, kept = refs[0], refs[1:5], refs[5 : 5 + carried]
    start_ref, send_ref, sems = refs[5 + carried :]
    slot_ref, cnbr_ref, csend_ref = kept[:3]
    held = (start_ref, send_ref, *kept)
    copies = [pltpu.make_async_copy(here, there, sems.at[i]) for i, (here, there) in enumerate(zip(given, held))]
    for copy in copies:
        copy.start()
    for copy in copies[:5]:
        copy.wait()
    rows, elements = start_ref.shape
    active = activity(counts_ref, elements)
    masked_ref[...] = jnp.where(active, start_ref[...], 0.0)
    index = pack(send_ref[...], masked_ref, outs, rows, elements)
    slots = rows8(jnp.where(active, slot_ref[...], -1).astype(jnp.float32))
    tiles = [slots[:, c : c + LANES] for c in range(0, elements, LANES)]
    csend = csend_ref[...].astype(jnp.float32)
    blank = jnp.zeros((1, LANES // 2 - csend.shape[1]), jnp.float32)
    order = ordered_sends(csend)
    table = cnbr_ref[...].astype(jnp.float32)
    table = jnp.concatenate([table, table], axis=1)
    halves = []
    for half in range(2):
        coarse = jnp.concatenate([order[2 * half], blank, order[2 * half + 1], blank], axis=1)
        halves.append(jnp.concatenate([pick(tiles, index[half])[0:1], coarse, table], axis=0))
    store_packets(outs, halves, rows)
    for copy in copies[5:]:
        copy.wait()


def local_blocks(current_ref, scale_ref, fscale_ref, nbr_ref, g_ref):
    rows, elements = current_ref.shape
    for c in range(0, elements, LANES):
        cols = slice(c, c + LANES)
        g_ref[0:rows, cols] = current_ref[:, cols] * scale_ref[:, cols]
    for face in range(FACES):
        for c in range(0, elements, LANES):
            cols = slice(c, c + LANES)
            entry = nbr_ref[face : face + 1, cols]
            here = (entry >= 0) & (entry < elements)
            weight = rows8(jnp.where(here, fscale_ref[face : face + 1, cols], 0.0))
            index = rows8(jnp.where(here, entry, 0))
            for row in range(0, rows, SUB):
                tiles = [current_ref[row : row + SUB, k : k + LANES] for k in range(0, elements, LANES)]
                at = rows * (face + 1) + row
                g_ref[at : at + SUB, cols] = weight * pick(tiles, index)


def ghost_tables(fscale_ref, nbr_ref, index_ref, early_ref, late_ref, sent):
    entry = nbr_ref[...] - fscale_ref.shape[1]
    way = jnp.maximum(entry, 0) // sent
    narrow = way // 2
    index_ref[...] = jnp.where(entry >= 0, narrow * sent + way * (-sent) + entry, 0)
    flips = []
    for axis in ("wide", "narrow"):
        even = lax.axis_size(axis) % 2 == 0
        flips.append(1 - lax.rem(lax.axis_index(axis), 2) if even else jnp.int32(0))
    swap = (way & 1) ^ jnp.where(narrow == 0, flips[0], flips[1])
    weight = jnp.where(entry >= 0, fscale_ref[...], 0.0)
    early_ref[...] = jnp.where(swap == 0, weight, 0.0)
    late_ref[...] = jnp.where(swap == 0, 0.0, weight)


def ghost_blocks(wide_ref, narrow_ref, rows, index_ref, weight_ref, g_ref, before_ref=None):
    halves = [
        jnp.concatenate([wide_ref[row : row + SUB, :], narrow_ref[row : row + SUB, :]], axis=1)
        for row in range(0, rows, SUB)
    ]
    for face in range(FACES):
        for c in range(0, index_ref.shape[1], LANES):
            cols = slice(c, c + LANES)
            weight = rows8(weight_ref[face : face + 1, cols])
            index = rows8(index_ref[face : face + 1, cols])
            for row in range(0, rows, SUB):
                at = rows * face + row
                value = weight * lane_take(halves[row // SUB], index)
                if before_ref is not None:
                    value = value + before_ref[at : at + SUB, cols]
                g_ref[at : at + SUB, cols] = value


def early_kernel(index_ref, weight_ref, wide_ref, narrow_ref, g_ref):
    ghost_blocks(wide_ref, narrow_ref, g_ref.shape[0] // FACES, index_ref, weight_ref, g_ref)


def first_local_kernel(
    counts_ref,
    start_ref,
    right_ref,
    scale_ref,
    fscale_ref,
    nbr_ref,
    elem_ref,
    smooth_ref,
    faces_ref,
    prolong_ref,
    csmooth_ref,
    part_ref,
    folded_ref,
    lead_ref,
    relax_ref,
    source_ref,
    index_ref,
    early_ref,
    late_ref,
    g_ref,
    *,
    sent,
):
    rows, elements = start_ref.shape
    ghost_tables(fscale_ref, nbr_ref, index_ref, early_ref, late_ref, sent)
    active = activity(counts_ref, elements)
    source_ref[...] = jnp.where(active, right_ref[...], 0.0)
    relax_ref[...] = jnp.where(active, OMEGA / scale_ref[...], 0.0)
    cdof = csmooth_ref.shape[0]
    lead_ref[rows:, :] = smooth_ref[...]
    for at in range(0, prolong_ref.shape[0], cdof):
        lead_ref[at : at + cdof, :] = dot(csmooth_ref[...], prolong_ref[at : at + cdof, :], HIGHEST)
    lead = lead_ref[...]
    folded_ref[:, 0:rows] = dot(lead, elem_ref[...], HIGHEST)
    for face in range(FACES):
        folded_ref[:, rows * (face + 1) : rows * (face + 2)] = dot(lead, faces_ref[face], HIGHEST)
    local_blocks(start_ref, scale_ref, fscale_ref, nbr_ref, g_ref)
    change = dot(smooth_ref[...], source_ref[...]) - dot(folded_ref[rows:, :], g_ref[...])
    part_ref[...] = start_ref[...] + relax_ref[...] * change


def smoothed_kernel(
    part_ref, relax_ref, folded_ref, index_ref, late_ref, early_ref, send_ref, p0, p1, p2, p3, smoothed_ref, *rest
):
    outs, g_ref = rest[:4], rest[4]
    rows, elements = part_ref.shape
    ghost_blocks(p1, p3, rows, index_ref, late_ref, g_ref, early_ref)
    smoothed_ref[...] = part_ref[...] - relax_ref[...] * dot(folded_ref[rows:, rows:], g_ref[...], HIGHEST)
    pack(send_ref[...], smoothed_ref, outs, rows, elements)
    packets = (p0, p1, p2, p3)
    for slot, axis in enumerate(("wide", "wide", "narrow", "narrow")):
        straight = slot if lax.axis_size(axis) % 2 else slot ^ 1
        relayed = (straight, 2, 3) if axis == "wide" else (straight,)
        for place, which in enumerate(relayed):
            at = rows + SUB * place
            outs[slot][at : at + SUB, :] = packets[which][rows : rows + SUB, :]


def second_local_kernel(
    counts_ref,
    smoothed_ref,
    source_ref,
    scale_ref,
    fscale_ref,
    nbr_ref,
    lead_ref,
    folded_ref,
    prolong_ref,
    slot_ref,
    cscale_ref,
    cfscale_ref,
    cnbr_ref,
    csend_ref,
    p0,
    p1,
    p2,
    p3,
    value_ref,
    spread_ref,
    prol_ref,
    place_ref,
    child_ref,
    weight_ref,
    table_ref,
    g_ref,
    *,
    kids,
):
    rows, elements = smoothed_ref.shape
    coarse = cscale_ref.shape[1]
    local_blocks(smoothed_ref, scale_ref, fscale_ref, nbr_ref, g_ref)
    value_ref[...] = dot(lead_ref[...], source_ref[...]) - dot(folded_ref[...], g_ref[...])

    prol_ref[...] = prolong_ref[...].T
    prol = prol_ref[...]
    for block in range(FACES + 1):
        cols = slice(rows * block, rows * (block + 1))
        spread_ref[:, cols] = dot(folded_ref[rows:, cols], prol)

    active = activity(counts_ref, elements)
    own = jnp.where(active, slot_ref[...], -1)
    halves = received((p0, p1, p2, p3), rows)
    tiles = [rows8(own[:, c : c + LANES].astype(jnp.float32)) for c in range(0, elements, LANES)]
    tiles += [rows8(half[0:1]) for half in halves]
    line = lax.broadcasted_iota(jnp.int32, (SUB, LANES), 0)
    blank = jnp.zeros((SUB - FACES, LANES), jnp.int32)
    side = halves[0].shape[1] // 2
    for c in range(0, elements, LANES):
        cols = slice(c, c + LANES)
        entry = jnp.concatenate([nbr_ref[:, cols], blank], axis=0)
        slot = pick(tiles, jnp.maximum(entry, 0)).astype(jnp.int32)
        slot = jnp.where(line == FACES, rows8(own[:, cols]), slot)
        live = (slot >= 0) & (entry >= 0)
        slot = jnp.where(live, slot, 0)
        group = jnp.where(entry >= elements, 1 + (entry - elements) // side, 0)
        place_ref[:, cols] = group * coarse + slot // kids
        child_ref[:, cols] = slot % kids
        weight = jnp.concatenate([fscale_ref[:, cols], scale_ref[:, cols], scale_ref[:, cols]], axis=0)
        weight_ref[:, cols] = jnp.where(live, weight, 0.0)

    cweight = jnp.where(cnbr_ref[...] >= 0, cfscale_ref[...] * (COARSE_OMEGA / cscale_ref[...]), 0.0)
    sends = jnp.concatenate([csend_ref[i : i + 1].astype(jnp.float32) for i in range(csend_ref.shape[0])], axis=1)
    spare = coarse - sends.shape[1]
    if spare:
        sends = jnp.concatenate([sends, jnp.zeros((1, spare), jnp.float32)], axis=1)
    table_ref[...] = jnp.concatenate([cweight, sends, sends], axis=0)


def restrict_kernel(
    value_ref,
    smoothed_ref,
    relax_ref,
    folded_ref,
    index_ref,
    late_ref,
    early_ref,
    slot_ref,
    cscale_ref,
    table_ref,
    wide_ref,
    narrow_ref,
    base_ref,
    message_ref,
    g_ref,
    *,
    kids,
):
    rows, elements = smoothed_ref.shape
    coarse = cscale_ref.shape[1]
    ghost_blocks(wide_ref, narrow_ref, rows, index_ref, late_ref, g_ref, early_ref)
    value = value_ref[...] - dot(folded_ref[:, rows:], g_ref[...])
    base_ref[...] = smoothed_ref[...] + relax_ref[...] * value[rows:, :]
    slot = slot_ref[...]
    child = rows8(slot % kids)
    step = rows // kids
    summed = jnp.where(child == 0, value[0:step, :], 0.0)
    for kid in range(1, kids):
        summed = jnp.where(child == kid, value[kid * step : (kid + 1) * step, :], summed)
    member = lax.broadcasted_iota(jnp.int32, (coarse, elements), 0) == slot // kids
    first = dot_t(summed, member.astype(jnp.float32)) * (COARSE_OMEGA / cscale_ref[...])
    message = jnp.concatenate([first, table_ref[...]], axis=1)
    for device in range(message_ref.shape[0]):
        message_ref[device] = message


def neighbourhood(mesh_shape, reach):
    wides, narrows = mesh_shape
    seen, found = set(), []
    near = [(0, 0), (-1, 0), (1, 0), (0, -1), (0, 1)]
    found.extend(near)
    seen.update((w % wides, n % narrows) for w, n in near)
    counts = [1, len(found)]
    for distance in range(2, reach + 1):
        for w in range(-distance, distance + 1):
            for n in (distance - abs(w), abs(w) - distance):
                key = (w % wides, n % narrows)
                if key not in seen:
                    seen.add(key)
                    found.append((w, n))
        counts.append(len(found))
    return found, counts


def neighbour_tables(row, own_ref, near, far):
    def brought(packets, axis, at):
        base = 0 if axis == "wide" else 2
        return in_order(axis, *(packet[at : at + SUB, :] for packet in packets[base : base + 2]))

    own = own_ref[...].astype(jnp.float32)
    found = {(0, 0): jnp.concatenate([jnp.zeros((SUB - FACES, own.shape[1]), jnp.float32), own], axis=0)}
    found[-1, 0], found[1, 0] = brought(near, "wide", row)
    found[0, -1], found[0, 1] = brought(near, "narrow", row)
    found[-2, 0], found[2, 0] = brought(far, "wide", row)
    found[0, -2], found[0, 2] = brought(far, "narrow", row)
    one, two = brought(far, "wide", row + SUB), brought(far, "wide", row + 2 * SUB)
    for side in range(2):
        found[2 * side - 1, -1], found[2 * side - 1, 1] = in_order("narrow", one[side], two[side])
    return found


def finish_kernel(
    message_ref,
    base_ref,
    relax_ref,
    prol_ref,
    spread_ref,
    place_ref,
    child_ref,
    weight_ref,
    cblock_ref,
    csmooth_ref,
    cfaces_ref,
    cnbr_ref,
    p0,
    p1,
    p2,
    p3,
    q0,
    q1,
    q2,
    q3,
    field_ref,
    correction_ref,
    folded_ref,
    cg_ref,
    g_ref,
    *,
    mesh_shape,
    kids,
    sent,
):
    rows, elements = base_ref.shape
    cdof, coarse = correction_ref.shape
    wides, narrows = mesh_shape
    offsets, counts = neighbourhood(mesh_shape, 3)
    parts = []
    for w, n in offsets:
        at_w = lax.rem(lax.axis_index("wide") + (w % wides), wides)
        at_n = lax.rem(lax.axis_index("narrow") + (n % narrows), narrows)
        parts.append(at_w * narrows + at_n)
    csmooth = csmooth_ref[...]
    own = COARSE_OMEGA * dot(csmooth, cblock_ref[...])
    for face in range(FACES):
        folded_ref[:, face * cdof : (face + 1) * cdof] = dot(csmooth, cfaces_ref[face])
    folded = folded_ref[...]

    tables = neighbour_tables(rows, cnbr_ref, (p0, p1, p2, p3), (q0, q1, q2, q3))
    ranks = {}
    for rank, (w, n) in reversed(list(enumerate(offsets))):
        ranks[w % wides, n % narrows] = rank
    beside = [[ranks[(w + dw) % wides, (n + dn) % narrows] for dw, dn in offsets[1:5]] for w, n in offsets[: counts[2]]]
    left = lax.broadcasted_iota(jnp.int32, (SUB, LANES), 1) < coarse
    straight = [message_ref[part] for part in parts]
    turned = [pltpu.roll(message, coarse, 1) for message in straight]

    def side_by_side(low, high, members, limit):
        kept = [rank if rank < limit else 0 for rank in members]
        kept += kept[:1] * (len(kept) % 2)
        return [jnp.where(left, low[a], high[b]) for a, b in zip(kept[::2], kept[1::2])]

    first, extras, around, indices = [], [], [], []
    for t in range(-(-counts[2] // 2)):
        pair = (2 * t, min(2 * t + 1, counts[2] - 1))
        first += side_by_side(straight, turned, pair, len(parts))
        extras += side_by_side(turned, straight, pair, len(parts))
        members = []
        for one in pair:
            for rank in (one, *beside[one]):
                if rank not in members:
                    members.append(rank)
        around.append(members)
        lists = [
            rows8(extra[FACES : FACES + 1]) for extra in side_by_side(turned, straight, members, len(parts))
        ]
        spots = [[members.index(rank) * coarse for rank in (one, *beside[one])] for one in pair]
        spots = [jnp.where(left, one, two) for one, two in zip(*spots)]
        entry = jnp.concatenate([tables[offsets[one]] for one in pair], axis=1)
        entry = jnp.maximum(entry.astype(jnp.int32), 0)
        remote = entry - coarse
        owner = jnp.where(
            remote < 2 * sent,
            jnp.where(remote < sent, spots[1], spots[2]),
            jnp.where(remote < 3 * sent, spots[3], spots[4]),
        )
        there = pick(lists, owner + jnp.maximum(remote, 0)).astype(jnp.int32)
        indices.append(jnp.where(remote < 0, spots[0] + entry, owner + there))

    low, high, current = straight, turned, first
    for count in (counts[2], counts[1]):
        tiles = -(-count // 2)
        for t in range(tiles):
            members = around[t]
            if 2 * t + 1 >= count:
                members = members[: 1 + len(set(beside[2 * t]) - {2 * t})]
            seen = side_by_side(low, high, members, len(low))
            for face in range(FACES):
                row = SUB - FACES + face
                chosen = pick(seen, rows8(indices[t][row : row + 1]))
                cg_ref[face * cdof : (face + 1) * cdof, t * LANES : (t + 1) * LANES] = (
                    rows8(extras[t][face : face + 1]) * chosen
                )
        pulled = dot(folded, cg_ref[:, : tiles * LANES])
        inner = dot(own, jnp.concatenate(current[:tiles], axis=1))
        following = []
        for t in range(tiles):
            cols = slice(t * LANES, (t + 1) * LANES)
            following.append(current[t] + first[t] - inner[:, cols] - pulled[:, cols])
        current = following
        flipped = [pltpu.roll(tile, coarse, 1) for tile in current]
        low = [tile for both in zip(current, flipped) for tile in both]
        high = [tile for both in zip(flipped, current) for tile in both]
    correction_ref[...] = current[0][:, :coarse]

    for c in range(0, elements, LANES):
        cols = slice(c, c + LANES)
        for row in range(FACES + 1):
            block = 0 if row == FACES else row + 1
            chosen = pick(current, rows8(place_ref[row : row + 1, cols]))
            child = rows8(child_ref[row : row + 1, cols])
            if row == FACES:
                live = rows8(jnp.where(weight_ref[row : row + 1, cols] > 0.0, 1.0, 0.0)) * chosen
                for kid in range(kids):
                    at = (FACES + 1) * rows + kid * cdof
                    g_ref[at : at + cdof, cols] = jnp.where(child == kid, live, 0.0)
            chosen = rows8(weight_ref[row : row + 1, cols]) * chosen
            for kid in range(kids):
                at = block * rows + kid * cdof
                g_ref[at : at + cdof, cols] = jnp.where(child == kid, chosen, 0.0)
    split = (FACES + 1) * rows
    change = dot(spread_ref[...], g_ref[0:split, :])
    delta = dot(prol_ref[...], g_ref[split:, :])
    field_ref[...] = base_ref[...] + delta - relax_ref[...] * change


def swap_routes(size):
    if size % 2:
        return [[(i, (i + 1) % size) for i in range(size)], [(i, (i - 1) % size) for i in range(size)]]
    return [
        [(i, i + 1 if i % 2 == 0 else i - 1) for i in range(size)],
        [(i, (i - 1 if i % 2 == 0 else i + 1) % size) for i in range(size)],
    ]


def exchange(packets):
    moved = []
    for base, axis in ((0, "wide"), (2, "narrow")):
        for half, route in enumerate(swap_routes(lax.axis_size(axis))):
            moved.append(lax.ppermute(packets[base + half], axis, route))
    return moved


SMEM = pl.BlockSpec(memory_space=pltpu.SMEM)
VMEM = pl.BlockSpec(memory_space=pltpu.VMEM)
HBM = pl.BlockSpec(memory_space=pltpu.HBM)


def call(kernel, scalars, arrays, shapes, scratch=(), flops=0, space=VMEM):
    outs = [jax.ShapeDtypeStruct(shape, dtype) for shape, dtype in shapes]
    if space is HBM:
        arrays = [pltpu.with_memory_space_constraint(x, pltpu.HBM) for x in arrays]
    moved = sum(x.size * 4 for x in arrays)
    return pl.pallas_call(
        kernel,
        out_shape=outs,
        in_specs=[SMEM] * len(scalars) + [space] * len(arrays),
        out_specs=[VMEM] * len(outs),
        scratch_shapes=[pltpu.VMEM(x, jnp.float32) if isinstance(x, tuple) else x for x in scratch],
        compiler_params=pltpu.CompilerParams(vmem_limit_bytes=GRANT),
        cost_estimate=pl.CostEstimate(flops=flops, bytes_accessed=moved, transcendentals=0),
    )(*scalars, *arrays)


def body(
    start_field,
    right_side,
    element_scale,
    face_scale,
    face_nbr,
    send_list,
    counts,
    coarse_slot,
    elem_block,
    smooth_block,
    face_blocks,
    prolong,
    coarse_scale,
    coarse_face_scale,
    coarse_nbr,
    coarse_send,
    coarse_block,
    coarse_smooth,
    coarse_faces,
):
    rows, elements = start_field.shape
    kids, _, cdof = prolong.shape
    prolong = prolong.transpose(0, 2, 1).reshape(kids * cdof, rows)
    coarse = coarse_scale.shape[0]
    sent = send_list.shape[1]
    mesh_shape = (lax.axis_size("wide"), lax.axis_size("narrow"))
    devices = mesh_shape[0] * mesh_shape[1]
    f32, i32 = jnp.float32, jnp.int32
    scale = element_scale.reshape(1, elements)
    slot = coarse_slot.reshape(1, elements)
    cscale = coarse_scale.reshape(1, coarse)
    blocks = (FACES + 1) * rows

    kept = (
        slot,
        coarse_nbr,
        coarse_send,
        right_side,
        scale,
        face_scale,
        face_nbr,
        elem_block,
        smooth_block,
        face_blocks,
        prolong,
        cscale,
        coarse_face_scale,
        coarse_block,
        coarse_smooth,
        coarse_faces,
        send_list,
    )
    start, *brought = call(
        functools.partial(start_kernel, carried=len(kept)),
        (counts,),
        (start_field, send_list, *kept),
        [((rows, elements), f32)] + [((rows + SUB, sent), f32)] * 4 + [(x.shape, x.dtype) for x in kept],
        [
            pltpu.VMEM(start_field.shape, f32),
            pltpu.VMEM(send_list.shape, i32),
            pltpu.SemaphoreType.DMA((len(kept) + 2,)),
        ],
        space=HBM,
    )
    packets = brought[:4]
    (
        slot,
        coarse_nbr,
        coarse_send,
        right_side,
        scale,
        face_scale,
        face_nbr,
        elem_block,
        smooth_block,
        face_blocks,
        prolong,
        cscale,
        coarse_face_scale,
        coarse_block,
        coarse_smooth,
        coarse_faces,
        send_list,
    ) = brought[4:]
    first_ghosts = exchange(packets)
    part, folded, lead, relax, source, ghost_index, early_weight, late_weight = call(
        functools.partial(first_local_kernel, sent=sent),
        (counts,),
        (
            start,
            right_side,
            scale,
            face_scale,
            face_nbr,
            elem_block,
            smooth_block,
            face_blocks,
            prolong,
            coarse_smooth,
        ),
        [
            ((rows, elements), f32),
            ((2 * rows, blocks), f32),
            ((2 * rows, rows), f32),
            ((1, elements), f32),
            ((rows, elements), f32),
            ((FACES, elements), i32),
            ((FACES, elements), f32),
            ((FACES, elements), f32),
        ],
        [(blocks, elements)],
        flops=2 * blocks * rows * elements,
    )
    early = call(
        early_kernel,
        (),
        (ghost_index, early_weight, first_ghosts[0], first_ghosts[2]),
        [((blocks - rows, elements), f32)],
        flops=blocks * elements,
    )[0]
    smoothed, *packets = call(
        smoothed_kernel,
        (),
        (part, relax, folded, ghost_index, late_weight, early, send_list, *first_ghosts),
        [((rows, elements), f32)] + [((rows + 3 * SUB, sent), f32)] * 2 + [((rows + SUB, sent), f32)] * 2,
        [(blocks - rows, elements)],
        flops=2 * blocks * rows * elements,
    )
    second_ghosts = exchange(packets)
    value, spread, prol, place, child, weight, table = call(
        functools.partial(second_local_kernel, kids=kids),
        (counts,),
        (
            smoothed,
            source,
            scale,
            face_scale,
            face_nbr,
            lead,
            folded,
            prolong,
            slot,
            cscale,
            coarse_face_scale,
            coarse_nbr,
            coarse_send,
            *first_ghosts,
        ),
        [
            ((2 * rows, elements), f32),
            ((rows, blocks), f32),
            ((rows, kids * cdof), f32),
            ((SUB, elements), i32),
            ((SUB, elements), i32),
            ((SUB, elements), f32),
            ((SUB, coarse), f32),
        ],
        [(blocks, elements)],
        flops=4 * blocks * rows * elements,
    )
    early = call(
        early_kernel,
        (),
        (ghost_index, early_weight, second_ghosts[0], second_ghosts[2]),
        [((blocks - rows, elements), f32)],
        flops=blocks * elements,
    )[0]
    base, message = call(
        functools.partial(restrict_kernel, kids=kids),
        (),
        (value, smoothed, relax, folded, ghost_index, late_weight, early, slot, cscale, table, second_ghosts[1], second_ghosts[3]),
        [((rows, elements), f32), ((devices, SUB, 2 * coarse), f32)],
        [(blocks - rows, elements)],
        flops=4 * blocks * rows * elements,
    )
    gathered = lax.all_to_all(message, ("wide", "narrow"), 0, 0)
    needed = -(-neighbourhood(mesh_shape, 3)[1][2] // 2) * 2 * coarse
    return tuple(
        call(
            functools.partial(finish_kernel, mesh_shape=mesh_shape, kids=kids, sent=coarse_send.shape[1]),
            (),
            (
                gathered,
                base,
                relax,
                prol,
                spread,
                place,
                child,
                weight,
                coarse_block,
                coarse_smooth,
                coarse_faces,
                coarse_nbr,
                *first_ghosts,
                *second_ghosts,
            ),
            [((rows, elements), f32), ((cdof, coarse), f32)],
            [(cdof, FACES * cdof), (FACES * cdof, needed), (blocks + rows, elements)],
            flops=2 * blocks * rows * elements,
        )
    )


def solution(mesh):
    both = ("wide", "narrow")

    return jax.shard_map(
        body,
        mesh=mesh,
        in_specs=(
            P(None, both),
            P(None, both),
            P(both),
            P(None, both),
            P(None, both),
            P(None, both),
            P(both),
            P(both),
            P(),
            P(),
            P(),
            P(),
            P(both),
            P(None, both),
            P(None, both),
            P(None, both),
            P(),
            P(),
            P(),
        ),
        out_specs=(P(None, both), P(None, both)),
        check_vma=False,
    )
```
